32 devices in a mesh: dp: 8 (over y, x, core), chan: 4 (over z).
Axes of the slice: x: 2, y: 2, z: 4, core: 2. Of those that a mesh axis runs over, the one named last changes fastest.
Arguments:
- inputs: bfloat16 [192, 152, 800], P('dp', None, 'chan'), may hold values from -6 to 6
- ocean_mask: int32 [192, 152], P('dp'), may hold values 0 or 1
- counts: int32 [4], replicated, may hold values from 1 to 2
- kernel: float32 [7, 7, 800], P(None, None, 'chan'), may hold values from -0.875 to 0.875
- conv_bias: float32 [800], P('chan'), may hold values from -3 to 3
- norm_gain: float32 [800], P('chan'), may hold values from 0.5 to 1.5
- norm_bias: float32 [800], P('chan'), may hold values from -3 to 3
- weight_in: bfloat16 [800, 3200], P(None, 'chan'), may hold values from -0.21875 to 0.21875
- bias_in: float32 [3200], P('chan'), may hold values from -3 to 3
- weight_out: bfloat16 [3200, 800], P('chan'), may hold values from -0.21875 to 0.21875
- bias_out: float32 [800], P('chan'), may hold values from -3 to 3
- cotangent: bfloat16 [192, 152, 800], P('dp', None, 'chan'), may hold values from -6 to 6
Outputs:
- output: bfloat16 [192, 152, 800], P('dp', None, 'chan')
- grad_inputs: float32 [192, 152, 800], P('dp', None, 'chan')
- grad_kernel: float32 [7, 7, 800], P(None, None, 'chan')
- grad_conv_bias: float32 [800], P('chan')
- grad_gain: float32 [800], P('chan')
- grad_norm_bias: float32 [800], P('chan')
- grad_weight_in: float32 [800, 3200], P(None, 'chan')
- grad_bias_in: float32 [3200], P('chan')
- grad_weight_out: float32 [3200, 800], P('chan')
- grad_bias_out: float32 [800], P('chan')
The draws below stay inside these ranges and needn't reach their ends.
All inputs are finite; a program needn't handle non-finite values. No bound on the sum of `ocean_mask` on one device may be relied on, other than what follows from the above.
Results may differ from the reference program's by a relative error of at most 0.0057.
Values may be sent and summed in bfloat16 or wider, within the bound.
No kernel may reach another device: no remote copies, remote signals or barrier semaphores. Data moves between devices by JAX's collectives and lax.ppermute only.
A program may use at most 192 MiB of HBM per device.

```python
import jax
import jax.numpy as jnp
from jax import lax

CH = 800
HIDDEN_SIZE = 3200
GROUPS = 8
HISTORY = 2
COLS = 152
SAMPLE_ROWS = 48
SAMPLES = 4
ROWS = 192


def plant(drawn, own_key, smallest, largest):
    spot = [jax.random.randint(jax.random.fold_in(own_key, axis), (), 0, length) for axis, length in enumerate(drawn.shape)]
    main_axis = drawn.shape.index(max(drawn.shape))
    beside = spot[:main_axis] + [(spot[main_axis] + 1) % drawn.shape[main_axis]] + spot[main_axis + 1:]
    return drawn.at[tuple(spot)].set(smallest).at[tuple(beside)].set(largest)


def level_of(own_key, shape, pieces, smallest, high):
    def one(position, blocks):
        heights = jax.random.uniform(jax.random.fold_in(jax.random.fold_in(own_key, 6), position), (blocks,), jnp.float32, smallest / len(pieces), high / len(pieces))
        return jnp.repeat(jnp.exp(heights), shape[position] // blocks).reshape((-1,) + (1,) * (len(shape) - position - 1))

    gain = one(*pieces[0])
    for cut in pieces[1:]:
        gain = gain * one(*cut)
    return gain


def noise(stream_key, dims, width, limit, shards=(), held_as=jnp.bfloat16):
    array = jax.random.normal(stream_key, dims, jnp.float32) * width
    if len(shards) > 0:
        array = level_of(stream_key, dims, shards, -0.22, 0.18) * array
    return jnp.clip(array, min=-limit, max=limit).astype(held_as)


def setup_inputs(seed: int = 0) -> dict:
    key_list = jax.random.split(jax.random.key(seed), 13)
    inputs = noise(key_list[0], (ROWS, COLS, CH), 1.0, 6.0, ((0, 8), (2, 4)))
    ocean_mask = plant((jax.random.randint(key_list[1], (ROWS, COLS), 0, 10) < 7).astype(jnp.int32), jax.random.fold_in(key_list[1], 1), 0, 1)
    counts = plant(jax.random.randint(key_list[2], (SAMPLES,), 1, 3), jax.random.fold_in(key_list[2], 1), 1, 2).astype(jnp.int32)
    kernel = noise(key_list[3], (7, 7, CH), 49 ** -0.5, 0.875, ((2, 4),), jnp.float32)
    conv_bias = noise(key_list[4], (CH,), 0.5, 3.0, ((0, 4),), jnp.float32)
    norm_gain = jnp.clip(0.5 + 1.0 * jax.random.uniform(key_list[5], (CH,), jnp.float32) ** level_of(key_list[5], (CH,), ((0, 4),), -0.2, 0.2), 0.5, 1.5)
    norm_bias = noise(key_list[6], (CH,), 0.5, 3.0, ((0, 4),), jnp.float32)
    weight_in = noise(key_list[7], (CH, HIDDEN_SIZE), CH ** -0.5, 0.21875, ((1, 4),))
    bias_in = noise(key_list[8], (HIDDEN_SIZE,), 0.5, 3.0, ((0, 4),), jnp.float32)
    weight_out = noise(key_list[9], (HIDDEN_SIZE, CH), (HIDDEN_SIZE // 4) ** -0.5, 0.21875, ((0, 4),))
    bias_out = noise(key_list[10], (CH,), 0.5, 3.0, ((0, 4),), jnp.float32)
    cotangent = noise(key_list[11], (ROWS, COLS, CH), 1.0, 6.0, ((0, 8), (2, 4)))
    return {"inputs": inputs, "ocean_mask": ocean_mask, "counts": counts, "kernel": kernel, "conv_bias": conv_bias, "norm_gain": norm_gain, "norm_bias": norm_bias, "weight_in": weight_in, "bias_in": bias_in, "weight_out": weight_out, "bias_out": bias_out, "cotangent": cotangent}


EPSILON = 1e-05

@jax.custom_vjp
def low(v):
    return lax.optimization_barrier(v.astype(jnp.bfloat16)).astype(jnp.float32)

@jax.custom_vjp
def low_back(v):
    return v

def low_keep(v):
    return (low(v), None)

def low_pass(kept, grad):
    return (grad,)

def back_keep(v):
    return (v, None)

def back_low(kept, grad):
    return (low(grad),)
low.defvjp(low_keep, low_pass)
low_back.defvjp(back_keep, back_low)

def depthwise(values, kernel):
    height = values.shape[1]
    across = values.shape[2]
    padded = jnp.pad(values, ((0, 0), (3, 3), (3, 3), (0, 0)))
    summed = jnp.zeros_like(values)
    for row_shift in range(7):
        for col_shift in range(7):
            summed = summed + padded[:, row_shift:row_shift + height, col_shift:col_shift + across, :] * kernel[row_shift, col_shift]
    return summed

def pointwise(normed, weight_in, bias_in, weight_out, bias_out):
    hidden = low_back(jnp.dot(normed, weight_in, precision=lax.Precision.HIGHEST) + bias_in)
    active = low(jax.nn.gelu(hidden, approximate=False))
    return low_back(jnp.dot(active, weight_out, precision=lax.Precision.HIGHEST) + bias_out)

def reference(inputs, ocean_mask, counts, kernel, conv_bias, norm_gain, norm_bias, weight_in, bias_in, weight_out, bias_out, cotangent):
    channel = jnp.arange(CH)
    history_keep = (channel[None, :] // (CH // HISTORY) < counts[:, None]).astype(jnp.float32)
    row_keep = jnp.repeat(history_keep, SAMPLE_ROWS, axis=0)[:, None, :]
    wet_cells = ocean_mask.astype(jnp.float32)[:, :, None]
    group_size = CH // GROUPS

    def forward(input_value, kernel_value, conv_value, gain_value, shift_value, win_value, bin_value, wout_value, bout_value):
        masked = input_value * wet_cells * row_keep
        convolved = depthwise(masked.reshape(SAMPLES, SAMPLE_ROWS, COLS, CH), kernel_value) + conv_value
        grouped = convolved.reshape(SAMPLES, SAMPLE_ROWS, COLS, GROUPS, group_size)
        centre = lax.optimization_barrier(jnp.mean(grouped, axis=(1, 2, 4), keepdims=True))
        spread = lax.optimization_barrier(jnp.mean((grouped - centre) ** 2, axis=(1, 2, 4), keepdims=True))
        standard = ((grouped - centre) * lax.rsqrt(spread + EPSILON)).reshape(ROWS, COLS, CH)
        normed = low(standard * gain_value + shift_value).reshape(SAMPLES, SAMPLE_ROWS * COLS, CH)

        def per_sample(block):
            return pointwise(block, win_value, bin_value, wout_value, bout_value)
        branch = lax.map(jax.checkpoint(per_sample), normed).reshape(ROWS, COLS, CH)
        return wet_cells * (masked + branch)
    result, pullback = jax.vjp(forward, inputs.astype(jnp.float32), kernel, conv_bias, norm_gain, norm_bias, weight_in.astype(jnp.float32), bias_in, weight_out.astype(jnp.float32), bias_out)
    grads = pullback(cotangent.astype(jnp.float32))
    return (result.astype(jnp.bfloat16), grads[0], grads[1], grads[2], grads[3], grads[4], grads[5], grads[6], grads[7], grads[8])
```

```python
import jax
import jax.numpy as jnp
from jax import lax
from jax.experimental import pallas as pl
from jax.experimental.pallas import tpu as pltpu
from jax.sharding import PartitionSpec as P

CH = 800
GROUPS = 8
HISTORY = 2
SPAN = 2
EPSILON = 1e-05
GROUP_SIZE = CH // GROUPS
PARTS = 4
ROW_BLOCK = 8
TILE = 256
F32 = jnp.float32
BF16 = jnp.bfloat16
VMEM = pl.BlockSpec(memory_space=pltpu.VMEM)
SMEM = pl.BlockSpec(memory_space=pltpu.SMEM)


def flipped(block, axis, bit):
    count = lax.axis_size(axis)
    return lax.ppermute(block, axis, [(place, place ^ bit) for place in range(count)])


def routed(block, allowed, partner):
    count, depth = lax.axis_size("dp"), lax.axis_size("chan")
    route = []
    for place in range(count):
        for level in range(depth):
            if allowed(place, level):
                to_place, to_level = partner(place, level)
                route.append((place * depth + level, to_place * depth + to_level))
    return lax.ppermute(block, ("dp", "chan"), route)


def lane_spans(channels):
    return [(start, min(128, channels - start)) for start in range(0, channels, 128)]


def by_lane_tile(rows):
    count, channels = rows.shape
    tiles = len(lane_spans(channels))
    padded = jnp.pad(rows, ((0, 0), (0, tiles * 128 - channels)))
    return padded.reshape(count, tiles, 128).transpose(1, 0, 2)


def frame(pad_ref, rim_ref, within, height, across, spans):
    top = jnp.where(within == 1, 0, height + 3)
    bottom = height + 3 - top
    for index in range(3):
        row = rim_ref[index].astype(F32)
        for tile, (start, width) in enumerate(spans):
            pad_ref[tile, top + index, 8 : 8 + across, 0:width] = row[:, start : start + width]
            pad_ref[tile, bottom + index] = jnp.zeros(pad_ref.shape[2:], F32)

    def sides(row, carry):
        for tile in range(len(spans)):
            pad_ref[tile, row, 0:8, :] = jnp.zeros((8, 128), F32)
            pad_ref[tile, row, 8 + across : 16 + across, :] = jnp.zeros((8, 128), F32)
        return carry

    lax.fori_loop(0, height + 6, sides, 0)


def depthwise_kernel(within_ref, x_ref, rim_ref, wet_ref, keep_ref, taps_ref, bias_ref, out_ref, stat_ref, pad_ref, sum_ref):
    height, across, channels = x_ref.shape
    spans = lane_spans(channels)
    frame(pad_ref, rim_ref, within_ref[0], height, across, spans)
    keep = keep_ref[...]

    def fill(row, carry):
        masked = x_ref[row].astype(F32) * wet_ref[row] * keep
        for tile, (start, width) in enumerate(spans):
            pad_ref[tile, row + 3, 8 : 8 + across, 0:width] = masked[:, start : start + width]
        return carry

    lax.fori_loop(0, height, fill, 0)
    sum_ref[...] = jnp.zeros_like(sum_ref)
    strips = across // 8
    for tile, (start, width) in enumerate(spans):

        def block(index, carry, tile=tile, start=start, width=width):
            row = index // strips * ROW_BLOCK
            col = pl.multiple_of(index % strips * 8, 8)
            acc = [jnp.broadcast_to(bias_ref[tile : tile + 1, :], (8, 128))] * ROW_BLOCK
            for b in range(7):
                rows = [pad_ref[tile, row + i, pl.ds(col + 5 + b, 8), :] for i in range(ROW_BLOCK + 6)]
                for a in range(7):
                    tap = jnp.broadcast_to(taps_ref[tile, a * 7 + b : a * 7 + b + 1, :], (8, 128))
                    for i in range(ROW_BLOCK):
                        acc[i] = acc[i] + rows[i + a] * tap
            total = acc[0]
            for i in range(ROW_BLOCK):
                out_ref[row + i, pl.ds(col, 8), start : start + width] = acc[i][:, :width]
                if i:
                    total = total + acc[i]
            sum_ref[tile] += total
            return carry

        lax.fori_loop(0, height // ROW_BLOCK * strips, block, 0)
    for tile, (start, width) in enumerate(spans):
        mean = jnp.sum(sum_ref[tile], axis=0, keepdims=True)[:, :width] / (height * across)

        def deviations(row, total, start=start, width=width, mean=mean):
            offset = out_ref[row, :, start : start + width] - mean
            return total + jnp.sum(offset * offset, axis=0, keepdims=True)

        stat_ref[0:1, start : start + width] = mean
        stat_ref[1:2, start : start + width] = lax.fori_loop(0, height, deviations, jnp.zeros((1, width), F32))


def depthwise(within, x, rim, wet, keep, taps, bias):
    height, across, channels = x.shape
    tiles = len(lane_spans(channels))
    return pl.pallas_call(
        depthwise_kernel,
        out_shape=(jax.ShapeDtypeStruct(x.shape, F32), jax.ShapeDtypeStruct((2, channels), F32)),
        in_specs=[SMEM] + [VMEM] * 6,
        out_specs=(VMEM, VMEM),
        scratch_shapes=[
            pltpu.VMEM((tiles, height + 6, across + 16, 128), F32),
            pltpu.VMEM((tiles, 8, 128), F32),
        ],
        compiler_params=pltpu.CompilerParams(vmem_limit_bytes=40 << 20),
        cost_estimate=pl.CostEstimate(flops=98 * x.size, bytes_accessed=6 * x.size, transcendentals=0),
        name="depthwise",
    )(within, x, rim, wet, keep, taps, bias)


def depthwise_back_kernel(
    within_ref, grad_ref, rim_ref, x_ref, cot_ref, wet_ref, keep_ref, taps_ref, out_ref, tap_grad_ref, pad_ref, acc_ref
):
    height, across, channels = x_ref.shape
    spans = lane_spans(channels)
    frame(pad_ref, rim_ref, within_ref[0], height, across, spans)

    def fill(row, carry):
        for tile, (start, width) in enumerate(spans):
            pad_ref[tile, row + 3, 8 : 8 + across, 0:width] = grad_ref[row, :, start : start + width]
        return carry

    lax.fori_loop(0, height, fill, 0)
    acc_ref[...] = jnp.zeros_like(acc_ref)
    strips = across // 8
    for tile, (start, width) in enumerate(spans):

        def block(index, carry, tile=tile, start=start, width=width):
            row = index // strips * ROW_BLOCK
            col = pl.multiple_of(index % strips * 8, 8)
            here = (pl.ds(col, 8), slice(start, start + width))
            keep = jnp.broadcast_to(keep_ref[0:1, start : start + width], (8, width))
            mask = [wet_ref[row + i, pl.ds(col, 8), :] * keep for i in range(ROW_BLOCK)]
            masked = [x_ref[row + i, here[0], here[1]].astype(F32) * mask[i] for i in range(ROW_BLOCK)]
            acc = [cot_ref[row + i, here[0], here[1]].astype(F32) for i in range(ROW_BLOCK)]
            for b in range(7):
                rows = [pad_ref[tile, row + i, pl.ds(col + 5 + b, 8), 0:width] for i in range(ROW_BLOCK + 6)]
                for a in range(7):
                    index_of_tap = (6 - a) * 7 + (6 - b)
                    tap = jnp.broadcast_to(taps_ref[tile, index_of_tap : index_of_tap + 1, 0:width], (8, width))
                    total = None
                    for i in range(ROW_BLOCK):
                        acc[i] = acc[i] + rows[i + a] * tap
                        product = rows[i + a] * masked[i]
                        total = product if total is None else total + product
                    acc_ref[tile, index_of_tap, :, 0:width] += total
            for i in range(ROW_BLOCK):
                out_ref[row + i, here[0], here[1]] = acc[i] * mask[i]
            return carry

        lax.fori_loop(0, height // ROW_BLOCK * strips, block, 0)
    for tile, (start, width) in enumerate(spans):
        tap_grad_ref[:, start : start + width] = jnp.sum(acc_ref[tile], axis=1)[:, 0:width]


def depthwise_back(within, grad, rim, x, cot, wet, keep, taps):
    height, across, channels = x.shape
    tiles = len(lane_spans(channels))
    return pl.pallas_call(
        depthwise_back_kernel,
        out_shape=(jax.ShapeDtypeStruct(x.shape, F32), jax.ShapeDtypeStruct((49, channels), F32)),
        in_specs=[SMEM] + [VMEM] * 7,
        out_specs=(VMEM, VMEM),
        scratch_shapes=[
            pltpu.VMEM((tiles, height + 6, across + 16, 128), F32),
            pltpu.VMEM((tiles, 49, 8, 128), F32),
        ],
        compiler_params=pltpu.CompilerParams(vmem_limit_bytes=50 << 20),
        cost_estimate=pl.CostEstimate(flops=196 * x.size, bytes_accessed=12 * x.size, transcendentals=0),
        name="depthwise_back",
    )(within, grad, rim, x, cot, wet, keep, taps)


def group_total(row):
    channels = row.shape[1]
    group = lax.broadcasted_iota(jnp.int32, (1, channels), 1) // GROUP_SIZE
    total = jnp.zeros((1, channels), F32)
    for index in range(channels // GROUP_SIZE):
        member = group == index
        total = jnp.where(member, jnp.sum(jnp.where(member, row, 0.0), axis=1, keepdims=True), total)
    return total


def cut_kernel(level_ref, cot_ref, wet_ref, *refs):
    blocks, bias_ref = refs[:PARTS], refs[PARTS]
    height, across, channels = cot_ref.shape
    rows = height // PARTS
    total = jnp.zeros((8, channels), F32)
    for k in range(PARTS):
        first = (level_ref[0] ^ k) * rows

        def one(row, total, k=k, first=first):
            grad = (cot_ref[first + row].astype(F32) * wet_ref[first + row]).astype(BF16)
            blocks[k][pl.ds(row * across, across), :] = grad
            return total + jnp.sum(grad.astype(F32).reshape(across // 8, 8, channels), axis=0)

        total = lax.fori_loop(0, rows, one, total)
    bias_ref[...] = jnp.sum(total, axis=0, keepdims=True)


def cut(level, cot, wet):
    height, across, channels = cot.shape
    block = jax.ShapeDtypeStruct((height // PARTS * across, channels), BF16)
    return pl.pallas_call(
        cut_kernel,
        out_shape=(block,) * PARTS + (jax.ShapeDtypeStruct((1, channels), F32),),
        in_specs=[SMEM, VMEM, VMEM],
        out_specs=(VMEM,) * (PARTS + 1),
        compiler_params=pltpu.CompilerParams(vmem_limit_bytes=30 << 20),
        cost_estimate=pl.CostEstimate(flops=2 * cot.size, bytes_accessed=4 * cot.size, transcendentals=0),
        name="cut",
    )(level, cot, wet)


def norm_kernel(level_ref, conv_ref, stat_ref, other_ref, gain_ref, bias_ref, *refs):
    blocks, fit_ref = refs[:PARTS], refs[PARTS]
    height, across, channels = conv_ref.shape
    rows = height // PARTS
    cells = height * across
    stat, other = stat_ref[...], other_ref[...]
    members = SPAN * GROUP_SIZE
    centre = group_total(stat[0:1] + other[0:1]) / members
    away, other_away = stat[0:1] - centre, other[0:1] - centre
    squares = stat[1:2] + other[1:2] + cells * (away * away + other_away * other_away)
    inverse = lax.rsqrt(group_total(squares) / (members * cells) + EPSILON)
    fit_ref[0:1] = centre
    fit_ref[1:2] = inverse
    gain, bias = gain_ref[...], bias_ref[...]
    for k in range(PARTS):
        first = (level_ref[0] ^ k) * rows

        def one(row, carry, k=k, first=first):
            standard = (conv_ref[first + row] - centre) * inverse
            blocks[k][pl.ds(row * across, across), :] = (standard * gain + bias).astype(BF16)
            return carry

        lax.fori_loop(0, rows, one, 0)


def norm(level, conv, stat, other, gain, bias):
    height, across, channels = conv.shape
    block = jax.ShapeDtypeStruct((height // PARTS * across, channels), BF16)
    return pl.pallas_call(
        norm_kernel,
        out_shape=(block,) * PARTS + (jax.ShapeDtypeStruct((2, channels), F32),),
        in_specs=[SMEM] + [VMEM] * 5,
        out_specs=(VMEM,) * (PARTS + 1),
        compiler_params=pltpu.CompilerParams(vmem_limit_bytes=30 << 20),
        cost_estimate=pl.CostEstimate(flops=4 * conv.size, bytes_accessed=6 * conv.size, transcendentals=0),
        name="norm",
    )(level, conv, stat, other, gain, bias)


def moments_kernel(level_ref, conv_ref, fit_ref, *refs):
    blocks, sums_ref = refs[:PARTS], refs[PARTS]
    height, across, channels = conv_ref.shape
    rows = height // PARTS
    centre, inverse = fit_ref[0:1], fit_ref[1:2]
    first_sum = jnp.zeros((8, channels), F32)
    second_sum = jnp.zeros((8, channels), F32)
    for k in range(PARTS):
        first = (level_ref[0] ^ k) * rows

        def one(row, sums, k=k, first=first):
            standard = (conv_ref[first + row] - centre) * inverse
            grad = blocks[k][pl.ds(row * across, across), :].astype(F32)
            fold = lambda v: jnp.sum(v.reshape(across // 8, 8, channels), axis=0)
            return sums[0] + fold(grad), sums[1] + fold(grad * standard)

        first_sum, second_sum = lax.fori_loop(0, rows, one, (first_sum, second_sum))
    sums_ref[0:1] = jnp.sum(first_sum, axis=0, keepdims=True)
    sums_ref[1:2] = jnp.sum(second_sum, axis=0, keepdims=True)


def moments(level, conv, fit, blocks):
    channels = conv.shape[2]
    return pl.pallas_call(
        moments_kernel,
        out_shape=jax.ShapeDtypeStruct((2, channels), F32),
        in_specs=[SMEM] + [VMEM] * (2 + PARTS),
        out_specs=VMEM,
        compiler_params=pltpu.CompilerParams(vmem_limit_bytes=30 << 20),
        cost_estimate=pl.CostEstimate(flops=6 * conv.size, bytes_accessed=6 * conv.size, transcendentals=0),
        name="moments",
    )(level, conv, fit, *blocks)


def norm_back_kernel(level_ref, within_ref, conv_ref, fit_ref, sums_ref, other_ref, gain_ref, *refs):
    blocks, (grad_ref, rim_ref, bias_ref) = refs[:PARTS], refs[PARTS:]
    height, across, channels = conv_ref.shape
    rows = height // PARTS
    members = SPAN * GROUP_SIZE * height * across
    centre, inverse = fit_ref[0:1], fit_ref[1:2]
    gain = gain_ref[...]
    sums = sums_ref[...] + other_ref[...]
    mean_first = group_total(sums[0:1] * gain) / members
    mean_second = group_total(sums[1:2] * gain) / members
    total = jnp.zeros((8, channels), F32)
    for k in range(PARTS):
        first = (level_ref[0] ^ k) * rows

        def one(row, total, k=k, first=first):
            standard = (conv_ref[first + row] - centre) * inverse
            grad = blocks[k][pl.ds(row * across, across), :].astype(F32)
            grad = inverse * (grad * gain - mean_first - standard * mean_second)
            grad_ref[first + row] = grad
            return total + jnp.sum(grad.reshape(across // 8, 8, channels), axis=0)

        total = lax.fori_loop(0, rows, one, total)
    bias_ref[...] = jnp.sum(total, axis=0, keepdims=True)
    edge = jnp.where(within_ref[0] == 0, height - 3, 0)
    for index in range(3):
        rim_ref[index] = grad_ref[edge + index].astype(BF16)


def norm_back(level, within, conv, fit, sums, other, gain, blocks):
    height, across, channels = conv.shape
    return pl.pallas_call(
        norm_back_kernel,
        out_shape=(
            jax.ShapeDtypeStruct(conv.shape, F32),
            jax.ShapeDtypeStruct((3, across, channels), BF16),
            jax.ShapeDtypeStruct((1, channels), F32),
        ),
        in_specs=[SMEM, SMEM] + [VMEM] * (5 + PARTS),
        out_specs=(VMEM,) * 3,
        compiler_params=pltpu.CompilerParams(vmem_limit_bytes=30 << 20),
        cost_estimate=pl.CostEstimate(flops=8 * conv.size, bytes_accessed=10 * conv.size, transcendentals=0),
        name="norm_back",
    )(level, within, conv, fit, sums, other, gain, *blocks)


def finish_kernel(level_ref, x_ref, wet_ref, keep_ref, bias_ref, *refs):
    blocks, out_ref = refs[:PARTS], refs[PARTS]
    height, across, channels = x_ref.shape
    rows = height // PARTS
    keep, bias = keep_ref[...], bias_ref[...]
    for k in range(PARTS):
        first = (level_ref[0] ^ k) * rows

        def one(row, carry, k=k, first=first):
            branch = blocks[k][pl.ds(row * across, across), :].astype(F32) + bias
            masked = x_ref[first + row].astype(F32) * keep
            out_ref[first + row] = (wet_ref[first + row] * (masked + branch)).astype(BF16)
            return carry

        lax.fori_loop(0, rows, one, 0)


def finish(level, x, wet, keep, bias, blocks):
    return pl.pallas_call(
        finish_kernel,
        out_shape=jax.ShapeDtypeStruct(x.shape, BF16),
        in_specs=[SMEM] + [VMEM] * (4 + PARTS),
        out_specs=VMEM,
        compiler_params=pltpu.CompilerParams(vmem_limit_bytes=30 << 20),
        cost_estimate=pl.CostEstimate(flops=4 * x.size, bytes_accessed=8 * x.size, transcendentals=0),
        name="finish",
    )(level, x, wet, keep, bias, *blocks)


def pointwise_kernel(twist_ref, *refs):
    acts = refs[: 4 * PARTS]
    win_ref, wout_ref, bias_ref = refs[4 * PARTS : 4 * PARTS + 3]
    outs = refs[4 * PARTS + 3 : 4 * PARTS + 11]
    grad_own_ref, grad_far_ref, own_ref, far_ref, in_keep_ref, in_send_ref, out_keep_ref, out_send_ref = outs
    turned_ref, turned_grad_ref, back_ref, branch_ref, hidden_ref, slope_ref, active_ref, grad_hidden_ref = refs[
        4 * PARTS + 11 :
    ]
    twist = twist_ref[0]
    cells, channels = acts[0].shape
    normed = (acts[:PARTS], acts[PARTS : 2 * PARTS])
    grads = (acts[2 * PARTS : 3 * PARTS], acts[3 * PARTS :])

    @pl.when(pl.program_id(0) == 0)
    def _():
        for side in range(2):
            for k in range(PARTS):
                turned_ref[side, k, 0:channels, :] = normed[side][k][...].T
                ones = (lax.broadcasted_iota(jnp.int32, (8, cells), 0) == 0).astype(BF16)
                turned_ref[side, k, channels : channels + 8, :] = ones
                turned_grad_ref[side, k] = grads[side][k][...].T
        back_ref[...] = jnp.zeros_like(back_ref)
        branch_ref[...] = jnp.zeros_like(branch_ref)

    for side in range(2):
        hidden = jnp.broadcast_to(bias_ref[...], (cells, TILE))
        grad = jnp.zeros((cells, TILE), F32)
        for k in range(PARTS):
            hidden = hidden + jnp.dot(normed[side][k][...], win_ref[twist ^ k], preferred_element_type=F32)
            grad = grad + jnp.dot(grads[side][k][...], wout_ref[twist ^ k], preferred_element_type=F32)
        hidden_ref[side] = hidden
        slope_ref[side] = grad
        value = hidden_ref[side]
        cumulative = 0.5 * (1.0 + lax.erf(value * 0.7071067811865476))
        density = jnp.exp(-0.5 * value * value) * 0.3989422804014327
        active_ref[side] = (value * cumulative).astype(BF16)
        grad_hidden_ref[side] = (slope_ref[side] * (cumulative + value * density)).astype(BF16)
        dims = (((1,), (1,)), ((), ()))
        for k in range(PARTS):
            branch_ref[side, k] += lax.dot_general(
                active_ref[side], wout_ref[twist ^ k], dims, preferred_element_type=F32
            )
            back_ref[side, k] += lax.dot_general(
                grad_hidden_ref[side], win_ref[twist ^ k], dims, preferred_element_type=F32
            )
    for j in range(PARTS):
        k = twist ^ j
        grad_in = jnp.dot(turned_ref[0, k], grad_hidden_ref[0], preferred_element_type=F32) + jnp.dot(
            turned_ref[1, k], grad_hidden_ref[1], preferred_element_type=F32
        )
        grad_out = jnp.dot(turned_grad_ref[0, k], active_ref[0], preferred_element_type=F32) + jnp.dot(
            turned_grad_ref[1, k], active_ref[1], preferred_element_type=F32
        )
        if j % 2 == 0:
            in_keep_ref[j // 2] = grad_in
        else:
            in_send_ref[j // 2] = grad_in.astype(BF16)
        if j < 2:
            out_keep_ref[j] = grad_out
        else:
            out_send_ref[j - 2] = grad_out.astype(BF16)

    @pl.when(pl.program_id(0) == pl.num_programs(0) - 1)
    def _():
        grad_own_ref[...] = back_ref[0].astype(BF16)
        grad_far_ref[...] = back_ref[1].astype(BF16)
        own_ref[...] = branch_ref[0].astype(BF16)
        far_ref[...] = branch_ref[1].astype(BF16)


def pointwise(twist, acts, win, wout, bias, units):
    cells, channels = acts[0].shape
    whole = lambda *shape: pl.BlockSpec(shape, lambda t: (0,) * len(shape), pipeline_mode=pl.Buffered(1))
    tiled = lambda *shape: pl.BlockSpec(shape + (TILE,), lambda t: (0,) * len(shape) + (t,))
    quad = jax.ShapeDtypeStruct((PARTS, cells, channels), BF16)
    return pl.pallas_call(
        pointwise_kernel,
        grid=(win.shape[2] // TILE,),
        out_shape=(quad,) * 4
        + (
            jax.ShapeDtypeStruct((2, channels + 8, units), F32),
            jax.ShapeDtypeStruct((2, channels + 8, units), BF16),
            jax.ShapeDtypeStruct((2, channels, units), F32),
            jax.ShapeDtypeStruct((2, channels, units), BF16),
        ),
        in_specs=[SMEM]
        + [whole(cells, channels)] * (4 * PARTS)
        + [tiled(PARTS, channels), tiled(PARTS, channels), tiled(1)],
        out_specs=(whole(PARTS, cells, channels),) * 4
        + (tiled(2, channels + 8), tiled(2, channels + 8), tiled(2, channels), tiled(2, channels)),
        scratch_shapes=[
            pltpu.VMEM((2, PARTS, channels + 8, cells), BF16),
            pltpu.VMEM((2, PARTS, channels, cells), BF16),
            pltpu.VMEM((2, PARTS, cells, channels), F32),
            pltpu.VMEM((2, PARTS, cells, channels), F32),
            pltpu.VMEM((2, cells, TILE), F32),
            pltpu.VMEM((2, cells, TILE), F32),
            pltpu.VMEM((2, cells, TILE), BF16),
            pltpu.VMEM((2, cells, TILE), BF16),
        ],
        compiler_params=pltpu.CompilerParams(vmem_limit_bytes=60 << 20, dimension_semantics=("arbitrary",)),
        cost_estimate=pl.CostEstimate(
            flops=24 * cells * PARTS * channels * units, bytes_accessed=40 << 20, transcendentals=4 * cells * units
        ),
        name="pointwise",
    )(twist, *acts, win, wout, bias)


def picked(stack, index):
    return lax.dynamic_index_in_dim(stack, index, 0, keepdims=False)


def body(
    inputs,
    ocean_mask,
    counts,
    kernel,
    conv_bias,
    norm_gain,
    norm_bias,
    weight_in,
    bias_in,
    weight_out,
    bias_out,
    cotangent,
):
    height, across, channels = inputs.shape
    units = weight_in.shape[1]
    place = lax.axis_index("dp")
    level = lax.axis_index("chan")
    core = place % SPAN
    quarter = place // SPAN % PARTS
    mine = level // 2 == core
    scalar = lambda value: value.astype(jnp.int32).reshape(1)
    core_of = lambda at: at % SPAN

    part = channels
    piece = jnp.stack(
        [
            lax.dynamic_slice_in_dim(weight_in, quarter * part, part, 0),
            lax.dynamic_slice_in_dim(weight_out, quarter * part, part, 1).T,
        ]
    )
    owner = lambda at, lev: lev // 2 == core_of(at)
    near = [
        tuple(
            routed(value, owner, lambda at, lev, k=k: (at, lev ^ k)) for value in (piece, bias_in.reshape(1, units))
        )
        for k in (1, 2, 3)
    ]
    first = [jnp.where(mine, own, far) for own, far in zip((piece, bias_in.reshape(1, units)), near[1])]
    second = [jnp.where(mine, one, far) for one, far in zip(near[0], near[2])]
    slab = jnp.concatenate([first[0], second[0]], axis=2)
    win_rows = [slab[0]]
    wout_rows = [slab[1]]
    win_rows += [flipped(win_rows[0], "dp", 2)]
    win_rows += [flipped(value, "dp", 4) for value in win_rows]
    across_wout = flipped(wout_rows[0], "dp", 4)
    wout_rows = [wout_rows[0], flipped(wout_rows[0], "dp", 2), across_wout, flipped(across_wout, "dp", 2)]
    room = -2 * units % TILE
    widen = lambda rows: jnp.pad(jnp.stack(rows), ((0, 0), (0, 0), (0, room)))
    win, wout = widen(win_rows), widen(wout_rows)
    bias_hidden = jnp.pad(jnp.concatenate([first[1], second[1]], axis=1), ((0, 0), (0, room)))

    sample = place // SPAN
    count_here = jnp.sum(jnp.where(jnp.arange(counts.shape[0]) == sample, counts, 0))
    channel = level * channels + jnp.arange(channels)
    keep = (channel // (CH // HISTORY) < count_here).astype(F32).reshape(1, channels)
    wet = ocean_mask.astype(F32)[:, :, None]
    edge = jnp.where(core == 0, height - 3, 0)
    outgoing = (
        lax.dynamic_slice_in_dim(inputs, edge, 3, 0).astype(F32) * lax.dynamic_slice_in_dim(wet, edge, 3, 0) * keep
    ).astype(BF16)
    rim = flipped(outgoing, "dp", 1)
    taps = by_lane_tile(kernel.reshape(49, channels))
    row = lambda vector: vector.reshape(1, channels)
    conv, stat = depthwise(scalar(core), inputs, rim, wet, keep, taps, by_lane_tile(row(conv_bias))[:, 0])
    *grad_blocks, grad_bias_out = cut(scalar(level), cotangent, wet)
    *normed_blocks, fit = norm(scalar(level), conv, stat, flipped(stat, "dp", 1), row(norm_gain), row(norm_bias))

    spread_out = lambda blocks: [blocks[0]] + [flipped(blocks[k], "chan", k) for k in range(1, PARTS)]
    grad_cells = spread_out(grad_blocks)
    normed_cells = spread_out(normed_blocks)
    other_core = lambda blocks: [flipped(block, "dp", 1) for block in blocks]
    acts = normed_cells + other_core(normed_cells) + grad_cells + other_core(grad_cells)
    back_own, back_far, branch_own, branch_far, in_keep, in_send, out_keep, out_send = pointwise(
        scalar(level ^ quarter), acts, win, wout, bias_hidden, 2 * units
    )
    joined = lambda own, far: [
        (own[k].astype(F32) + far[k].astype(F32)).astype(BF16) for k in range(PARTS)
    ]
    back_blocks = spread_out(joined(back_own, flipped(back_far, "dp", 1)))
    branch_blocks = spread_out(joined(branch_own, flipped(branch_far, "dp", 1)))

    sums = moments(scalar(level), conv, fit, back_blocks)
    grad_conv, outgoing_grad, grad_conv_bias = norm_back(
        scalar(level), scalar(core), conv, fit, sums, flipped(sums, "dp", 1), row(norm_gain), back_blocks
    )
    grad_rim = flipped(outgoing_grad, "dp", 1)
    grad_inputs, grad_taps = depthwise_back(scalar(core), grad_conv, grad_rim, inputs, cotangent, wet, keep, taps)
    output = finish(scalar(level), inputs, wet, keep, row(bias_out), branch_blocks)
    small = jnp.concatenate([grad_taps, grad_conv_bias, sums[1:2], sums[0:1], grad_bias_out, jnp.zeros((3, channels), F32)])
    bit = 1
    while bit < lax.axis_size("dp"):
        small = small + flipped(small, "dp", bit)
        bit *= 2

    wide = lambda value: value.astype(F32)
    in_two = in_keep + wide(flipped(in_send, "dp", 2))
    out_two = out_keep + wide(flipped(out_send, "dp", 4))
    in_one = in_two[0] + wide(flipped(in_two[1].astype(BF16), "dp", 4))
    out_one = out_two[0] + wide(flipped(out_two[1].astype(BF16), "dp", 2))
    both = jnp.concatenate([in_one, out_one])
    low = both.astype(BF16)
    stranger = lambda at, lev: not owner(at, lev)
    total = (
        both[:, :units]
        + wide(routed(low[:, units:], owner, lambda at, lev: (at, lev ^ 1)))
        + wide(routed(low[:, :units], stranger, lambda at, lev: (at, lev ^ 2)))
        + wide(routed(low[:, units:], stranger, lambda at, lev: (at, lev ^ 3)))
    )
    bit = SPAN * PARTS
    while bit < lax.axis_size("dp"):
        total = total + flipped(total, "dp", bit)
        bit *= 2
    held = total.astype(BF16)
    held = jnp.where(mine, held, flipped(held, "dp", 1))
    share = jnp.where(core == 0, held[: channels + 8], jnp.pad(held[channels + 8 :], ((0, 8), (0, 0))))
    always = lambda at, lev: True
    turn = lambda value, step: routed(value, always, lambda at, lev: (at ^ (2 << (core_of(at) ^ step)), lev))
    one = turn(share, 0)
    two = turn(share, 1)
    three = turn(one, 1)
    shares = jnp.stack([share, jnp.where(core == 0, one, two), jnp.where(core == 0, two, one), three])
    others = flipped(shares, "dp", 1)
    in_shares = jnp.where(core == 0, shares, others)
    out_shares = jnp.where(core == 0, others, shares)
    ordered_in = [picked(in_shares, quarter ^ c) for c in range(PARTS)]
    ordered_out = [picked(out_shares, quarter ^ c)[:channels] for c in range(PARTS)]
    grad_weight_in = jnp.concatenate([value[:channels] for value in ordered_in]).astype(F32)
    grad_weight_out = jnp.concatenate(ordered_out).astype(F32).T
    grad_bias_in = ordered_in[0][channels].astype(F32)
    return (
        output,
        grad_inputs,
        small[:49].reshape(7, 7, channels),
        small[49],
        small[50],
        small[51],
        grad_weight_in,
        grad_bias_in,
        grad_weight_out,
        small[52],
    )


def solution(mesh):
    in_specs = (
        P("dp", None, "chan"),
        P("dp", None),
        P(),
        P(None, None, "chan"),
        P("chan"),
        P("chan"),
        P("chan"),
        P(None, "chan"),
        P("chan"),
        P("chan", None),
        P("chan"),
        P("dp", None, "chan"),
    )
    out_specs = (
        P("dp", None, "chan"),
        P("dp", None, "chan"),
        P(None, None, "chan"),
        P("chan"),
        P("chan"),
        P("chan"),
        P(None, "chan"),
        P("chan"),
        P("chan", None),
        P("chan"),
    )
    return jax.shard_map(body, mesh=mesh, in_specs=in_specs, out_specs=out_specs, check_vma=False)
```

```python
import jax
import jax.numpy as jnp
from jax import lax
from jax.experimental import pallas as pl
from jax.experimental.pallas import tpu as pltpu
from jax.sharding import PartitionSpec as P

CH = 800
GROUPS = 8
HISTORY = 2
SPAN = 2
EPSILON = 1e-05
GROUP_SIZE = CH // GROUPS
PARTS = 4
ROW_BLOCK = 8
TILE = 256
F32 = jnp.float32
BF16 = jnp.bfloat16
VMEM = pl.BlockSpec(memory_space=pltpu.VMEM)
SMEM = pl.BlockSpec(memory_space=pltpu.SMEM)


def flipped(block, axis, bit):
    count = lax.axis_size(axis)
    return lax.ppermute(block, axis, [(place, place ^ bit) for place in range(count)])


def routed(block, allowed, partner):
    count, depth = lax.axis_size("dp"), lax.axis_size("chan")
    route = []
    for place in range(count):
        for level in range(depth):
            if allowed(place, level):
                to_place, to_level = partner(place, level)
                route.append((place * depth + level, to_place * depth + to_level))
    return lax.ppermute(block, ("dp", "chan"), route)


def lane_spans(channels):
    return [(start, min(128, channels - start)) for start in range(0, channels, 128)]


def by_lane_tile(rows):
    count, channels = rows.shape
    tiles = len(lane_spans(channels))
    padded = jnp.pad(rows, ((0, 0), (0, tiles * 128 - channels)))
    return padded.reshape(count, tiles, 128).transpose(1, 0, 2)


def frame(pad_ref, rim_ref, within, height, across, spans):
    top = jnp.where(within == 1, 0, height + 3)
    bottom = height + 3 - top
    for index in range(3):
        row = rim_ref[index].astype(F32)
        for tile, (start, width) in enumerate(spans):
            pad_ref[tile, top + index, 8 : 8 + across, 0:width] = row[:, start : start + width]
            pad_ref[tile, bottom + index] = jnp.zeros(pad_ref.shape[2:], F32)

    def sides(row, carry):
        for tile in range(len(spans)):
            pad_ref[tile, row, 0:8, :] = jnp.zeros((8, 128), F32)
            pad_ref[tile, row, 8 + across : 16 + across, :] = jnp.zeros((8, 128), F32)
        return carry

    lax.fori_loop(0, height + 6, sides, 0)


def depthwise_kernel(within_ref, x_ref, rim_ref, wet_ref, keep_ref, taps_ref, bias_ref, out_ref, stat_ref, pad_ref, sum_ref):
    height, across, channels = x_ref.shape
    spans = lane_spans(channels)
    frame(pad_ref, rim_ref, within_ref[0], height, across, spans)
    keep = keep_ref[...]

    def fill(row, carry):
        masked = x_ref[row].astype(F32) * wet_ref[row] * keep
        for tile, (start, width) in enumerate(spans):
            pad_ref[tile, row + 3, 8 : 8 + across, 0:width] = masked[:, start : start + width]
        return carry

    lax.fori_loop(0, height, fill, 0)
    sum_ref[...] = jnp.zeros_like(sum_ref)
    strips = across // 8
    for tile, (start, width) in enumerate(spans):

        def block(index, carry, tile=tile, start=start, width=width):
            row = index // strips * ROW_BLOCK
            col = pl.multiple_of(index % strips * 8, 8)
            acc = [jnp.broadcast_to(bias_ref[tile : tile + 1, :], (8, 128))] * ROW_BLOCK
            for b in range(7):
                rows = [pad_ref[tile, row + i, pl.ds(col + 5 + b, 8), :] for i in range(ROW_BLOCK + 6)]
                for a in range(7):
                    tap = jnp.broadcast_to(taps_ref[tile, a * 7 + b : a * 7 + b + 1, :], (8, 128))
                    for i in range(ROW_BLOCK):
                        acc[i] = acc[i] + rows[i + a] * tap
            total = acc[0]
            for i in range(ROW_BLOCK):
                out_ref[row + i, pl.ds(col, 8), start : start + width] = acc[i][:, :width]
                if i:
                    total = total + acc[i]
            sum_ref[tile] += total
            return carry

        lax.fori_loop(0, height // ROW_BLOCK * strips, block, 0)
    for tile, (start, width) in enumerate(spans):
        mean = jnp.sum(sum_ref[tile], axis=0, keepdims=True)[:, :width] / (height * across)

        def deviations(row, total, start=start, width=width, mean=mean):
            offset = out_ref[row, :, start : start + width] - mean
            return total + jnp.sum(offset * offset, axis=0, keepdims=True)

        stat_ref[0:1, start : start + width] = mean
        stat_ref[1:2, start : start + width] = lax.fori_loop(0, height, deviations, jnp.zeros((1, width), F32))


def depthwise(within, x, rim, wet, keep, taps, bias):
    height, across, channels = x.shape
    tiles = len(lane_spans(channels))
    return pl.pallas_call(
        depthwise_kernel,
        out_shape=(jax.ShapeDtypeStruct(x.shape, F32), jax.ShapeDtypeStruct((2, channels), F32)),
        in_specs=[SMEM] + [VMEM] * 6,
        out_specs=(VMEM, VMEM),
        scratch_shapes=[
            pltpu.VMEM((tiles, height + 6, across + 16, 128), F32),
            pltpu.VMEM((tiles, 8, 128), F32),
        ],
        compiler_params=pltpu.CompilerParams(vmem_limit_bytes=40 << 20),
        cost_estimate=pl.CostEstimate(flops=98 * x.size, bytes_accessed=6 * x.size, transcendentals=0),
        name="depthwise",
    )(within, x, rim, wet, keep, taps, bias)


def depthwise_back_kernel(
    within_ref, grad_ref, rim_ref, x_ref, cot_ref, wet_ref, keep_ref, taps_ref, out_ref, tap_grad_ref, pad_ref, acc_ref
):
    height, across, channels = x_ref.shape
    spans = lane_spans(channels)
    frame(pad_ref, rim_ref, within_ref[0], height, across, spans)

    def fill(row, carry):
        for tile, (start, width) in enumerate(spans):
            pad_ref[tile, row + 3, 8 : 8 + across, 0:width] = grad_ref[row, :, start : start + width]
        return carry

    lax.fori_loop(0, height, fill, 0)
    acc_ref[...] = jnp.zeros_like(acc_ref)
    strips = across // 8
    for tile, (start, width) in enumerate(spans):

        def block(index, carry, tile=tile, start=start, width=width):
            row = index // strips * ROW_BLOCK
            col = pl.multiple_of(index % strips * 8, 8)
            here = (pl.ds(col, 8), slice(start, start + width))
            keep = jnp.broadcast_to(keep_ref[0:1, start : start + width], (8, width))
            mask = [wet_ref[row + i, pl.ds(col, 8), :] * keep for i in range(ROW_BLOCK)]
            masked = [x_ref[row + i, here[0], here[1]].astype(F32) * mask[i] for i in range(ROW_BLOCK)]
            acc = [cot_ref[row + i, here[0], here[1]].astype(F32) for i in range(ROW_BLOCK)]
            for b in range(7):
                rows = [pad_ref[tile, row + i, pl.ds(col + 5 + b, 8), 0:width] for i in range(ROW_BLOCK + 6)]
                for a in range(7):
                    index_of_tap = (6 - a) * 7 + (6 - b)
                    tap = jnp.broadcast_to(taps_ref[tile, index_of_tap : index_of_tap + 1, 0:width], (8, width))
                    total = None
                    for i in range(ROW_BLOCK):
                        acc[i] = acc[i] + rows[i + a] * tap
                        product = rows[i + a] * masked[i]
                        total = product if total is None else total + product
                    acc_ref[tile, index_of_tap, :, 0:width] += total
            for i in range(ROW_BLOCK):
                out_ref[row + i, here[0], here[1]] = acc[i] * mask[i]
            return carry

        lax.fori_loop(0, height // ROW_BLOCK * strips, block, 0)
    for tile, (start, width) in enumerate(spans):
        tap_grad_ref[:, start : start + width] = jnp.sum(acc_ref[tile], axis=1)[:, 0:width]


def depthwise_back(within, grad, rim, x, cot, wet, keep, taps):
    height, across, channels = x.shape
    tiles = len(lane_spans(channels))
    return pl.pallas_call(
        depthwise_back_kernel,
        out_shape=(jax.ShapeDtypeStruct(x.shape, F32), jax.ShapeDtypeStruct((49, channels), F32)),
        in_specs=[SMEM] + [VMEM] * 7,
        out_specs=(VMEM, VMEM),
        scratch_shapes=[
            pltpu.VMEM((tiles, height + 6, across + 16, 128), F32),
            pltpu.VMEM((tiles, 49, 8, 128), F32),
        ],
        compiler_params=pltpu.CompilerParams(vmem_limit_bytes=50 << 20),
        cost_estimate=pl.CostEstimate(flops=196 * x.size, bytes_accessed=12 * x.size, transcendentals=0),
        name="depthwise_back",
    )(within, grad, rim, x, cot, wet, keep, taps)


def group_total(row):
    channels = row.shape[1]
    group = lax.broadcasted_iota(jnp.int32, (1, channels), 1) // GROUP_SIZE
    total = jnp.zeros((1, channels), F32)
    for index in range(channels // GROUP_SIZE):
        member = group == index
        total = jnp.where(member, jnp.sum(jnp.where(member, row, 0.0), axis=1, keepdims=True), total)
    return total


def cut_kernel(level_ref, cot_ref, wet_ref, *refs):
    blocks, bias_ref = refs[:PARTS], refs[PARTS]
    height, across, channels = cot_ref.shape
    rows = height // PARTS
    total = jnp.zeros((8, channels), F32)
    for k in range(PARTS):
        first = (level_ref[0] ^ k) * rows

        def one(row, total, k=k, first=first):
            grad = (cot_ref[first + row].astype(F32) * wet_ref[first + row]).astype(BF16)
            blocks[k][pl.ds(row * across, across), :] = grad
            return total + jnp.sum(grad.astype(F32).reshape(across // 8, 8, channels), axis=0)

        total = lax.fori_loop(0, rows, one, total)
    bias_ref[...] = jnp.sum(total, axis=0, keepdims=True)


def cut(level, cot, wet):
    height, across, channels = cot.shape
    block = jax.ShapeDtypeStruct((height // PARTS * across, channels), BF16)
    return pl.pallas_call(
        cut_kernel,
        out_shape=(block,) * PARTS + (jax.ShapeDtypeStruct((1, channels), F32),),
        in_specs=[SMEM, VMEM, VMEM],
        out_specs=(VMEM,) * (PARTS + 1),
        compiler_params=pltpu.CompilerParams(vmem_limit_bytes=30 << 20),
        cost_estimate=pl.CostEstimate(flops=2 * cot.size, bytes_accessed=4 * cot.size, transcendentals=0),
        name="cut",
    )(level, cot, wet)


def norm_kernel(level_ref, conv_ref, stat_ref, other_ref, gain_ref, bias_ref, *refs):
    blocks, fit_ref = refs[:PARTS], refs[PARTS]
    height, across, channels = conv_ref.shape
    rows = height // PARTS
    cells = height * across
    stat, other = stat_ref[...], other_ref[...]
    members = SPAN * GROUP_SIZE
    centre = group_total(stat[0:1] + other[0:1]) / members
    away, other_away = stat[0:1] - centre, other[0:1] - centre
    squares = stat[1:2] + other[1:2] + cells * (away * away + other_away * other_away)
    inverse = lax.rsqrt(group_total(squares) / (members * cells) + EPSILON)
    fit_ref[0:1] = centre
    fit_ref[1:2] = inverse
    gain, bias = gain_ref[...], bias_ref[...]
    for k in range(PARTS):
        first = (level_ref[0] ^ k) * rows

        def one(row, carry, k=k, first=first):
            standard = (conv_ref[first + row] - centre) * inverse
            blocks[k][pl.ds(row * across, across), :] = (standard * gain + bias).astype(BF16)
            return carry

        lax.fori_loop(0, rows, one, 0)


def norm(level, conv, stat, other, gain, bias):
    height, across, channels = conv.shape
    block = jax.ShapeDtypeStruct((height // PARTS * across, channels), BF16)
    return pl.pallas_call(
        norm_kernel,
        out_shape=(block,) * PARTS + (jax.ShapeDtypeStruct((2, channels), F32),),
        in_specs=[SMEM] + [VMEM] * 5,
        out_specs=(VMEM,) * (PARTS + 1),
        compiler_params=pltpu.CompilerParams(vmem_limit_bytes=30 << 20),
        cost_estimate=pl.CostEstimate(flops=4 * conv.size, bytes_accessed=6 * conv.size, transcendentals=0),
        name="norm",
    )(level, conv, stat, other, gain, bias)


def moments_kernel(level_ref, conv_ref, fit_ref, *refs):
    blocks, sums_ref = refs[:PARTS], refs[PARTS]
    height, across, channels = conv_ref.shape
    rows = height // PARTS
    centre, inverse = fit_ref[0:1], fit_ref[1:2]
    first_sum = jnp.zeros((8, channels), F32)
    second_sum = jnp.zeros((8, channels), F32)
    for k in range(PARTS):
        first = (level_ref[0] ^ k) * rows

        def one(row, sums, k=k, first=first):
            standard = (conv_ref[first + row] - centre) * inverse
            grad = blocks[k][pl.ds(row * across, across), :].astype(F32)
            fold = lambda v: jnp.sum(v.reshape(across // 8, 8, channels), axis=0)
            return sums[0] + fold(grad), sums[1] + fold(grad * standard)

        first_sum, second_sum = lax.fori_loop(0, rows, one, (first_sum, second_sum))
    sums_ref[0:1] = jnp.sum(first_sum, axis=0, keepdims=True)
    sums_ref[1:2] = jnp.sum(second_sum, axis=0, keepdims=True)


def moments(level, conv, fit, blocks):
    channels = conv.shape[2]
    return pl.pallas_call(
        moments_kernel,
        out_shape=jax.ShapeDtypeStruct((2, channels), F32),
        in_specs=[SMEM] + [VMEM] * (2 + PARTS),
        out_specs=VMEM,
        compiler_params=pltpu.CompilerParams(vmem_limit_bytes=30 << 20),
        cost_estimate=pl.CostEstimate(flops=6 * conv.size, bytes_accessed=6 * conv.size, transcendentals=0),
        name="moments",
    )(level, conv, fit, *blocks)


def norm_back_kernel(level_ref, within_ref, conv_ref, fit_ref, sums_ref, other_ref, gain_ref, *refs):
    blocks, (grad_ref, rim_ref, bias_ref) = refs[:PARTS], refs[PARTS:]
    height, across, channels = conv_ref.shape
    rows = height // PARTS
    members = SPAN * GROUP_SIZE * height * across
    centre, inverse = fit_ref[0:1], fit_ref[1:2]
    gain = gain_ref[...]
    sums = sums_ref[...] + other_ref[...]
    mean_first = group_total(sums[0:1] * gain) / members
    mean_second = group_total(sums[1:2] * gain) / members
    total = jnp.zeros((8, channels), F32)
    for k in range(PARTS):
        first = (level_ref[0] ^ k) * rows

        def one(row, total, k=k, first=first):
            standard = (conv_ref[first + row] - centre) * inverse
            grad = blocks[k][pl.ds(row * across, across), :].astype(F32)
            grad = inverse * (grad * gain - mean_first - standard * mean_second)
            grad_ref[first + row] = grad
            return total + jnp.sum(grad.reshape(across // 8, 8, channels), axis=0)

        total = lax.fori_loop(0, rows, one, total)
    bias_ref[...] = jnp.sum(total, axis=0, keepdims=True)
    edge = jnp.where(within_ref[0] == 0, height - 3, 0)
    for index in range(3):
        rim_ref[index] = grad_ref[edge + index].astype(BF16)


def norm_back(level, within, conv, fit, sums, other, gain, blocks):
    height, across, channels = conv.shape
    return pl.pallas_call(
        norm_back_kernel,
        out_shape=(
            jax.ShapeDtypeStruct(conv.shape, F32),
            jax.ShapeDtypeStruct((3, across, channels), BF16),
            jax.ShapeDtypeStruct((1, channels), F32),
        ),
        in_specs=[SMEM, SMEM] + [VMEM] * (5 + PARTS),
        out_specs=(VMEM,) * 3,
        compiler_params=pltpu.CompilerParams(vmem_limit_bytes=30 << 20),
        cost_estimate=pl.CostEstimate(flops=8 * conv.size, bytes_accessed=10 * conv.size, transcendentals=0),
        name="norm_back",
    )(level, within, conv, fit, sums, other, gain, *blocks)


def finish_kernel(level_ref, x_ref, wet_ref, keep_ref, bias_ref, *refs):
    blocks, out_ref = refs[:PARTS], refs[PARTS]
    height, across, channels = x_ref.shape
    rows = height // PARTS
    keep, bias = keep_ref[...], bias_ref[...]
    for k in range(PARTS):
        first = (level_ref[0] ^ k) * rows

        def one(row, carry, k=k, first=first):
            branch = blocks[k][pl.ds(row * across, across), :].astype(F32) + bias
            masked = x_ref[first + row].astype(F32) * keep
            out_ref[first + row] = (wet_ref[first + row] * (masked + branch)).astype(BF16)
            return carry

        lax.fori_loop(0, rows, one, 0)


def finish(level, x, wet, keep, bias, blocks):
    return pl.pallas_call(
        finish_kernel,
        out_shape=jax.ShapeDtypeStruct(x.shape, BF16),
        in_specs=[SMEM] + [VMEM] * (4 + PARTS),
        out_specs=VMEM,
        compiler_params=pltpu.CompilerParams(vmem_limit_bytes=30 << 20),
        cost_estimate=pl.CostEstimate(flops=4 * x.size, bytes_accessed=8 * x.size, transcendentals=0),
        name="finish",
    )(level, x, wet, keep, bias, *blocks)


TURNED = (((1,), (1,)), ((), ()))


def forward_kernel(twist_ref, *refs):
    acts = refs[: 2 * PARTS]
    win_ref, wout_ref, bias_ref, own_ref, far_ref, active_ref, slope_ref, turned_ref, branch_ref, hidden_ref = refs[
        2 * PARTS :
    ]
    twist = twist_ref[0]
    cells, channels = acts[0].shape

    @pl.when(pl.program_id(0) == 0)
    def _():
        for side in range(2):
            for k in range(PARTS):
                turned_ref[side, k, 0:channels, :] = acts[side * PARTS + k][...].T
                ones = (lax.broadcasted_iota(jnp.int32, (8, cells), 0) == 0).astype(BF16)
                turned_ref[side, k, channels : channels + 8, :] = ones
        branch_ref[...] = jnp.zeros_like(branch_ref)

    for side in range(2):
        hidden = jnp.broadcast_to(bias_ref[...], (cells, TILE))
        for k in range(PARTS):
            hidden = hidden + jnp.dot(
                acts[side * PARTS + k][...], win_ref[twist ^ k], preferred_element_type=F32
            )
        hidden_ref[side] = hidden
        value = hidden_ref[side]
        cumulative = 0.5 * (1.0 + lax.erf(value * 0.7071067811865476))
        density = jnp.exp(-0.5 * value * value) * 0.3989422804014327
        active_ref[side] = (value * cumulative).astype(BF16)
        slope_ref[side] = cumulative + value * density
        for k in range(PARTS):
            branch_ref[side, k] += lax.dot_general(
                active_ref[side], wout_ref[twist ^ k], TURNED, preferred_element_type=F32
            )

    @pl.when(pl.program_id(0) == pl.num_programs(0) - 1)
    def _():
        own_ref[...] = branch_ref[0].astype(BF16)
        far_ref[...] = branch_ref[1].astype(BF16)


def whole(*shape):
    return pl.BlockSpec(shape, lambda t: (0,) * len(shape), pipeline_mode=pl.Buffered(1))


def tiled(*shape):
    return pl.BlockSpec(shape + (TILE,), lambda t: (0,) * len(shape) + (t,))


def forward(twist, acts, win, wout, bias):
    cells, channels = acts[0].shape
    units = win.shape[2]
    quad = jax.ShapeDtypeStruct((PARTS, cells, channels), BF16)
    return pl.pallas_call(
        forward_kernel,
        grid=(units // TILE,),
        out_shape=(
            quad,
            quad,
            jax.ShapeDtypeStruct((2, cells, units), BF16),
            jax.ShapeDtypeStruct((2, cells, units), F32),
            jax.ShapeDtypeStruct((2, PARTS, channels + 8, cells), BF16),
        ),
        in_specs=[SMEM]
        + [whole(cells, channels)] * (2 * PARTS)
        + [tiled(PARTS, channels), tiled(PARTS, channels), tiled(1)],
        out_specs=(
            whole(PARTS, cells, channels),
            whole(PARTS, cells, channels),
            tiled(2, cells),
            tiled(2, cells),
            whole(2, PARTS, channels + 8, cells),
        ),
        scratch_shapes=[
            pltpu.VMEM((2, PARTS, cells, channels), F32),
            pltpu.VMEM((2, cells, TILE), F32),
        ],
        compiler_params=pltpu.CompilerParams(vmem_limit_bytes=60 << 20, dimension_semantics=("arbitrary",)),
        cost_estimate=pl.CostEstimate(
            flops=8 * cells * PARTS * channels * units, bytes_accessed=32 << 20, transcendentals=4 * cells * units
        ),
        name="forward",
    )(twist, *acts, win, wout, bias)


def backward_kernel(twist_ref, *refs):
    grads = refs[: 2 * PARTS]
    turned_ref, win_ref, wout_ref, active_ref, slope_ref = refs[2 * PARTS : 2 * PARTS + 5]
    own_ref, far_ref, in_keep_ref, in_send_ref, out_keep_ref, out_send_ref = refs[2 * PARTS + 5 : 2 * PARTS + 11]
    turned_grad_ref, back_ref, grad_hidden_ref = refs[2 * PARTS + 11 :]
    twist = twist_ref[0]
    cells, channels = grads[0].shape

    @pl.when(pl.program_id(0) == 0)
    def _():
        for side in range(2):
            for k in range(PARTS):
                turned_grad_ref[side, k] = grads[side * PARTS + k][...].T
        back_ref[...] = jnp.zeros_like(back_ref)

    for side in range(2):
        grad = jnp.zeros((cells, TILE), F32)
        for k in range(PARTS):
            grad = grad + jnp.dot(
                grads[side * PARTS + k][...], wout_ref[twist ^ k], preferred_element_type=F32
            )
        grad_hidden_ref[side] = (grad * slope_ref[side]).astype(BF16)
        for k in range(PARTS):
            back_ref[side, k] += lax.dot_general(
                grad_hidden_ref[side], win_ref[twist ^ k], TURNED, preferred_element_type=F32
            )
    for j in range(PARTS):
        k = twist ^ j
        grad_in = jnp.dot(turned_ref[0, k], grad_hidden_ref[0], preferred_element_type=F32) + jnp.dot(
            turned_ref[1, k], grad_hidden_ref[1], preferred_element_type=F32
        )
        grad_out = jnp.dot(turned_grad_ref[0, k], active_ref[0], preferred_element_type=F32) + jnp.dot(
            turned_grad_ref[1, k], active_ref[1], preferred_element_type=F32
        )
        if j % 2 == 0:
            in_keep_ref[j // 2] = grad_in
        else:
            in_send_ref[j // 2] = grad_in.astype(BF16)
        if j < 2:
            out_keep_ref[j] = grad_out
        else:
            out_send_ref[j - 2] = grad_out.astype(BF16)

    @pl.when(pl.program_id(0) == pl.num_programs(0) - 1)
    def _():
        own_ref[...] = back_ref[0].astype(BF16)
        far_ref[...] = back_ref[1].astype(BF16)


def backward(twist, grads, turned, win, wout, active, slope, units):
    cells, channels = grads[0].shape
    quad = jax.ShapeDtypeStruct((PARTS, cells, channels), BF16)
    return pl.pallas_call(
        backward_kernel,
        grid=(win.shape[2] // TILE,),
        out_shape=(
            quad,
            quad,
            jax.ShapeDtypeStruct((2, channels + 8, units), F32),
            jax.ShapeDtypeStruct((2, channels + 8, units), BF16),
            jax.ShapeDtypeStruct((2, channels, units), F32),
            jax.ShapeDtypeStruct((2, channels, units), BF16),
        ),
        in_specs=[SMEM]
        + [whole(cells, channels)] * (2 * PARTS)
        + [
            whole(2, PARTS, channels + 8, cells),
            tiled(PARTS, channels),
            tiled(PARTS, channels),
            tiled(2, cells),
            tiled(2, cells),
        ],
        out_specs=(
            whole(PARTS, cells, channels),
            whole(PARTS, cells, channels),
            tiled(2, channels + 8),
            tiled(2, channels + 8),
            tiled(2, channels),
            tiled(2, channels),
        ),
        scratch_shapes=[
            pltpu.VMEM((2, PARTS, channels, cells), BF16),
            pltpu.VMEM((2, PARTS, cells, channels), F32),
            pltpu.VMEM((2, cells, TILE), BF16),
        ],
        compiler_params=pltpu.CompilerParams(vmem_limit_bytes=60 << 20, dimension_semantics=("arbitrary",)),
        cost_estimate=pl.CostEstimate(
            flops=16 * cells * PARTS * channels * units, bytes_accessed=50 << 20, transcendentals=0
        ),
        name="backward",
    )(twist, *grads, turned, win, wout, active, slope)


def join_kernel(own_ref, far_ref, *blocks):
    for k in range(PARTS):
        blocks[k][...] = (own_ref[k].astype(F32) + far_ref[k].astype(F32)).astype(BF16)


def join(own, far):
    block = jax.ShapeDtypeStruct(own.shape[1:], BF16)
    return pl.pallas_call(
        join_kernel,
        out_shape=(block,) * PARTS,
        in_specs=[VMEM, VMEM],
        out_specs=(VMEM,) * PARTS,
        compiler_params=pltpu.CompilerParams(vmem_limit_bytes=30 << 20),
        cost_estimate=pl.CostEstimate(flops=own.size, bytes_accessed=6 * own.size, transcendentals=0),
        name="join",
    )(own, far)


def gather_kernel(place_ref, *refs):
    near, far = refs[:PARTS], refs[PARTS : 2 * PARTS]
    in_ref, out_ref, bias_ref, held_ref = refs[2 * PARTS :]
    core, quarter = place_ref[0], place_ref[1]
    for shares, holder in ((near, core), (far, 1 - core)):
        for step, share in enumerate(shares):
            turn = (0, 1 << holder, 2 >> holder, 3)[step]
            held_ref[holder, quarter ^ turn] = share[...]
    channels = in_ref.shape[0] // PARTS
    for c in range(PARTS):
        in_ref[c * channels : (c + 1) * channels, :] = held_ref[0, c, 0:channels, :].astype(F32)
        out_ref[:, c * channels : (c + 1) * channels] = held_ref[1, c, 0:channels, :].astype(F32).T
    bias_ref[...] = held_ref[0, 0, channels : channels + 8, :].astype(F32)[0:1]


def gather(place, near, far, channels):
    rows, units = near[0].shape
    return pl.pallas_call(
        gather_kernel,
        out_shape=(
            jax.ShapeDtypeStruct((PARTS * channels, units), F32),
            jax.ShapeDtypeStruct((units, PARTS * channels), F32),
            jax.ShapeDtypeStruct((1, units), F32),
        ),
        in_specs=[SMEM] + [VMEM] * (2 * PARTS),
        out_specs=(VMEM,) * 3,
        scratch_shapes=[pltpu.VMEM((2, PARTS, rows, units), BF16)],
        compiler_params=pltpu.CompilerParams(vmem_limit_bytes=40 << 20),
        cost_estimate=pl.CostEstimate(flops=0, bytes_accessed=12 * PARTS * rows * units, transcendentals=0),
        name="gather",
    )(place, *near, *far)


def after(value, *earlier):
    return lax.optimization_barrier((value, earlier))[0]


def body(
    inputs,
    ocean_mask,
    counts,
    kernel,
    conv_bias,
    norm_gain,
    norm_bias,
    weight_in,
    bias_in,
    weight_out,
    bias_out,
    cotangent,
):
    height, across, channels = inputs.shape
    units = weight_in.shape[1]
    place = lax.axis_index("dp")
    level = lax.axis_index("chan")
    core = place % SPAN
    quarter = place // SPAN % PARTS
    mine = level // 2 == core
    scalar = lambda value: value.astype(jnp.int32).reshape(1)
    core_of = lambda at: at % SPAN

    part = channels
    piece = jnp.stack(
        [
            lax.dynamic_slice_in_dim(weight_in, quarter * part, part, 0),
            lax.dynamic_slice_in_dim(weight_out, quarter * part, part, 1).T,
        ]
    )
    rest = bias_in.reshape(1, units)
    digits = []
    for _ in range(3):
        digits.append(lax.reduce_precision(rest, 8, 7))
        rest = rest - digits[-1]
    piece = jnp.concatenate(
        [piece.reshape(2 * part, units)] + [digit.astype(BF16) for digit in digits] + [jnp.zeros((5, units), BF16)]
    )
    owner = lambda at, lev: lev // 2 == core_of(at)
    near = [routed(piece, owner, lambda at, lev, k=k: (at, lev ^ k)) for k in (1, 2, 3)]
    slab = jnp.concatenate([jnp.where(mine, piece, near[1]), jnp.where(mine, near[0], near[2])], axis=1)
    win_rows = [slab[:part]]
    wout_rows = [slab[part : 2 * part]]
    win_rows += [flipped(win_rows[0], "dp", 2)]
    win_rows += [flipped(value, "dp", 4) for value in win_rows]
    across_wout = flipped(wout_rows[0], "dp", 4)
    wout_rows = [wout_rows[0], flipped(wout_rows[0], "dp", 2), across_wout, flipped(across_wout, "dp", 2)]
    room = -2 * units % TILE
    widen = lambda rows: jnp.pad(jnp.stack(rows), ((0, 0), (0, 0), (0, room)))
    win, wout = widen(win_rows), widen(wout_rows)
    digits = slab[2 * part : 2 * part + 3].astype(F32)
    bias_hidden = jnp.pad(digits[0:1] + digits[1:2] + digits[2:3], ((0, 0), (0, room)))

    sample = place // SPAN
    count_here = jnp.sum(jnp.where(jnp.arange(counts.shape[0]) == sample, counts, 0))
    channel = level * channels + jnp.arange(channels)
    keep = (channel // (CH // HISTORY) < count_here).astype(F32).reshape(1, channels)
    wet = ocean_mask.astype(F32)[:, :, None]
    edge = jnp.where(core == 0, height - 3, 0)
    outgoing = (
        lax.dynamic_slice_in_dim(inputs, edge, 3, 0).astype(F32) * lax.dynamic_slice_in_dim(wet, edge, 3, 0) * keep
    ).astype(BF16)
    rim = flipped(outgoing, "dp", 1)
    taps = by_lane_tile(kernel.reshape(49, channels))
    row = lambda vector: vector.reshape(1, channels)
    conv, stat = depthwise(scalar(core), inputs, rim, wet, keep, taps, by_lane_tile(row(conv_bias))[:, 0])
    *normed_blocks, fit = norm(scalar(level), conv, stat, flipped(stat, "dp", 1), row(norm_gain), row(norm_bias))
    *grad_blocks, grad_bias_out = cut(scalar(level), after(cotangent, normed_blocks), wet)

    spread_out = lambda blocks: [blocks[0]] + [flipped(blocks[k], "chan", k) for k in range(1, PARTS)]
    other_core = lambda blocks: [flipped(block, "dp", 1) for block in blocks]
    twist = scalar(level ^ quarter)
    normed_cells = spread_out(normed_blocks)
    grad_cells = spread_out(after(grad_blocks, normed_cells))
    branch_own, branch_far, active, slope, turned = forward(
        twist, normed_cells + other_core(normed_cells), win, wout, bias_hidden
    )
    branch_blocks = join(branch_own, flipped(branch_far, "dp", 1))
    back_own, back_far, in_keep, in_send, out_keep, out_send = backward(
        twist, grad_cells + other_core(grad_cells), turned, win, wout, active, slope, 2 * units
    )
    joined = join(back_own, flipped(back_far, "dp", 1))
    branch_blocks = spread_out(after(branch_blocks, grad_cells))
    back_blocks = spread_out(joined)

    sums = moments(scalar(level), conv, fit, back_blocks)
    grad_conv, outgoing_grad, grad_conv_bias = norm_back(
        scalar(level), scalar(core), conv, fit, sums, flipped(sums, "dp", 1), row(norm_gain), back_blocks
    )
    grad_rim = flipped(outgoing_grad, "dp", 1)
    grad_inputs, grad_taps = depthwise_back(scalar(core), grad_conv, grad_rim, inputs, cotangent, wet, keep, taps)
    small = jnp.concatenate([grad_taps, grad_conv_bias, sums[1:2], sums[0:1], grad_bias_out, jnp.zeros((3, channels), F32)])
    bit = 1
    while bit < lax.axis_size("dp"):
        small = small + flipped(small, "dp", bit)
        bit *= 2

    wide = lambda value: value.astype(F32)
    in_send, out_send = after((in_send, out_send), joined)
    in_two = in_keep + wide(flipped(in_send, "dp", 2))
    out_two = out_keep + wide(flipped(out_send, "dp", 4))
    in_one = in_two[0] + wide(flipped(in_two[1].astype(BF16), "dp", 4))
    out_one = out_two[0] + wide(flipped(out_two[1].astype(BF16), "dp", 2))
    both = jnp.concatenate([in_one, out_one])
    low = after(both.astype(BF16), back_blocks)
    stranger = lambda at, lev: not owner(at, lev)
    arrived = (
        routed(low[:, units:], owner, lambda at, lev: (at, lev ^ 1)),
        routed(low[:, :units], stranger, lambda at, lev: (at, lev ^ 2)),
        routed(low[:, units:], stranger, lambda at, lev: (at, lev ^ 3)),
    )
    output = finish(scalar(level), inputs, wet, keep, row(bias_out), branch_blocks)
    arrived = after(arrived, grad_taps)
    total = both[:, :units] + wide(arrived[0]) + wide(arrived[1]) + wide(arrived[2])
    bit = SPAN * PARTS
    while bit < lax.axis_size("dp"):
        total = total + flipped(total, "dp", bit)
        bit *= 2
    held = total.astype(BF16)
    held = jnp.where(mine, held, flipped(held, "dp", 1))
    share = jnp.where(core == 0, held[: part + 8], jnp.pad(held[part + 8 :], ((0, 8), (0, 0))))
    always = lambda at, lev: True
    turn = lambda value, step: routed(value, always, lambda at, lev: (at ^ (2 << (core_of(at) ^ step)), lev))
    one = turn(share, 0)
    shares = [share, one, turn(share, 1), turn(one, 1)]
    grad_weight_in, grad_weight_out, grad_bias_in = gather(
        jnp.stack([core, quarter]).astype(jnp.int32), shares, other_core(shares), part
    )
    return (
        output,
        grad_inputs,
        small[:49].reshape(7, 7, channels),
        small[49],
        small[50],
        small[51],
        grad_weight_in,
        grad_bias_in.reshape(units),
        grad_weight_out,
        small[52],
    )


def solution(mesh):
    in_specs = (
        P("dp", None, "chan"),
        P("dp", None),
        P(),
        P(None, None, "chan"),
        P("chan"),
        P("chan"),
        P("chan"),
        P(None, "chan"),
        P("chan"),
        P("chan", None),
        P("chan"),
        P("dp", None, "chan"),
    )
    out_specs = (
        P("dp", None, "chan"),
        P("dp", None, "chan"),
        P(None, None, "chan"),
        P("chan"),
        P("chan"),
        P("chan"),
        P(None, "chan"),
        P("chan"),
        P("chan", None),
        P("chan"),
    )
    return jax.shard_map(body, mesh=mesh, in_specs=in_specs, out_specs=out_specs, check_vma=False)
```

```python
import jax
import jax.numpy as jnp
from jax import lax
from jax.experimental import pallas as pl
from jax.experimental.pallas import tpu as pltpu
from jax.sharding import PartitionSpec as P

CH = 800
GROUPS = 8
HISTORY = 2
SPAN = 2
EPSILON = 1e-05
GROUP_SIZE = CH // GROUPS
PARTS = 4
HALVES = 2
STEPS = 4
CHUNKS = 3
TILE = 256
COST = pl.CostEstimate(flops=4096, bytes_accessed=4096, transcendentals=0)
LANES = 256
F32 = jnp.float32
BF16 = jnp.bfloat16
VMEM = pl.BlockSpec(memory_space=pltpu.VMEM)
SMEM = pl.BlockSpec(memory_space=pltpu.SMEM)


def flipped(block, axis, bit):
    count = lax.axis_size(axis)
    return lax.ppermute(block, axis, [(place, place ^ bit) for place in range(count)])


def routed(block, allowed, partner):
    count, depth = lax.axis_size("dp"), lax.axis_size("chan")
    route = []
    for place in range(count):
        for level in range(depth):
            if allowed(place, level):
                to_place, to_level = partner(place, level)
                route.append((place * depth + level, to_place * depth + to_level))
    return lax.ppermute(block, ("dp", "chan"), route)


def lane_spans(channels):
    return [(start, min(128, channels - start)) for start in range(0, channels, 128)]


def by_lane_tile(rows):
    count, channels = rows.shape
    tiles = len(lane_spans(channels))
    padded = jnp.pad(rows, ((0, 0), (0, tiles * 128 - channels)))
    return padded.reshape(count, tiles, 128).transpose(1, 0, 2)


def summed(terms):
    while len(terms) > 1:
        terms = [terms[i] + terms[i + 1] for i in range(0, len(terms) - 1, 2)] + terms[len(terms) & ~1 :]
    return terms[0]


def fill_frame(pad_ref, rim_ref, within, first, height, across, spans, load):
    rows = pad_ref.shape[1]

    def store(at, row):
        for tile, (start, width) in enumerate(spans):
            pad_ref[tile, at, 8 : 8 + across, 0:width] = row[:, start : start + width]

    inner = [at for at in range(rows) if 0 <= first - 3 + at < height]

    def fill(at, carry):
        store(at, load(at + first - 3))
        return carry

    lax.fori_loop(inner[0], inner[-1] + 1, fill, 0)
    for at in range(rows):
        source = first - 3 + at
        if source < 0:
            store(at, rim_ref[source + 3].astype(F32) * (within == 1).astype(F32))
        elif source >= height:
            store(at, rim_ref[source - height].astype(F32) * (within == 0).astype(F32))

    def sides(at, carry):
        for tile in range(len(spans)):
            pad_ref[tile, at, 0:8, :] = jnp.zeros((8, 128), F32)
            pad_ref[tile, at, 8 + across : 16 + across, :] = jnp.zeros((8, 128), F32)
        return carry

    lax.fori_loop(0, rows, sides, 0)


def depthwise_kernel(half, within_ref, x_ref, rim_ref, wet_ref, keep_ref, taps_ref, bias_ref, *refs):
    before_ref = refs[0] if half else None
    out_ref, stat_ref, pad_ref, sum_ref = refs[half:]
    height, across, channels = x_ref.shape
    rows = height // HALVES
    row_block = rows
    spans = lane_spans(channels)
    keep = keep_ref[...]
    load = lambda row: x_ref[row].astype(F32) * wet_ref[row] * keep
    fill_frame(pad_ref, rim_ref, within_ref[0], half * rows, height, across, spans, load)
    sum_ref[...] = jnp.zeros_like(sum_ref)
    strips = across // 8
    for tile, (start, width) in enumerate(spans):

        def block(index, carry, tile=tile, start=start, width=width):
            row = index // strips * row_block
            col = pl.multiple_of(index % strips * 8, 8)
            acc = [jnp.broadcast_to(bias_ref[tile : tile + 1, :], (8, 128))] * row_block
            for b in range(7):
                lines = [pad_ref[tile, row + i, pl.ds(col + 5 + b, 8), :] for i in range(row_block + 6)]
                tap = [jnp.broadcast_to(taps_ref[tile, a * 7 + b : a * 7 + b + 1, :], (8, 128)) for a in range(7)]
                for i in range(row_block):
                    acc[i] = acc[i] + summed([lines[i + a] * tap[a] for a in range(7)])
            total = acc[0]
            for i in range(row_block):
                out_ref[row + i, pl.ds(col, 8), start : start + width] = acc[i][:, :width]
                if i:
                    total = total + acc[i]
            sum_ref[tile] += total
            return carry

        lax.fori_loop(0, rows // row_block * strips, block, 0)
    cells = rows * across
    for tile, (start, width) in enumerate(spans):
        mean = jnp.sum(sum_ref[tile], axis=0, keepdims=True)[:, :width] / cells

        def deviations(row, total, start=start, width=width, mean=mean):
            offset = out_ref[row, :, start : start + width] - mean
            return total + jnp.sum((offset * offset).reshape(strips, 8, width), axis=0)

        squares = lax.fori_loop(0, rows, deviations, jnp.zeros((8, width), F32))
        squares = jnp.sum(squares, axis=0, keepdims=True)
        if half:
            other = before_ref[0:1, start : start + width]
            squares = squares + before_ref[1:2, start : start + width] + (mean - other) * (mean - other) * (cells / 2)
            mean = 0.5 * (mean + other)
        stat_ref[0:1, start : start + width] = mean
        stat_ref[1:2, start : start + width] = squares


def depthwise(half, within, x, rim, wet, keep, taps, bias, *before):
    height, across, channels = x.shape
    rows = height // HALVES
    tiles = len(lane_spans(channels))

    def kernel(*refs):
        depthwise_kernel(half, *refs)

    return pl.pallas_call(
        kernel,
        out_shape=(
            jax.ShapeDtypeStruct((rows, across, channels), F32),
            jax.ShapeDtypeStruct((2, channels), F32),
        ),
        in_specs=[SMEM] + [VMEM] * (6 + half),
        out_specs=(VMEM, VMEM),
        scratch_shapes=[
            pltpu.VMEM((tiles, rows + 6, across + 16, 128), F32),
            pltpu.VMEM((tiles, 8, 128), F32),
        ],
        compiler_params=pltpu.CompilerParams(vmem_limit_bytes=16 << 20),
        cost_estimate=COST,
        name="depthwise" + "ab"[half],
    )(within, x, rim, wet, keep, taps, bias, *before)


def depthwise_back_kernel(step, within_ref, grad_ref, rim_ref, x_ref, cot_ref, wet_ref, keep_ref, taps_ref, *refs):
    out_ref, tap_grad_ref, pad_ref, acc_ref = refs[2 * (step > 0) :]
    height, across, channels = grad_ref.shape
    rows = height // STEPS
    row_block = rows
    spans = lane_spans(channels)
    fill_frame(pad_ref, rim_ref, within_ref[0], step * rows, height, across, spans, lambda row: grad_ref[row])
    acc_ref[...] = jnp.zeros_like(acc_ref)
    strips = across // 8
    for tile, (start, width) in enumerate(spans):

        def block(index, carry, tile=tile, start=start, width=width):
            row = index // strips * row_block
            col = pl.multiple_of(index % strips * 8, 8)
            here = (pl.ds(col, 8), slice(start, start + width))
            keep = jnp.broadcast_to(keep_ref[0:1, start : start + width], (8, width))
            mask = [wet_ref[row + i, pl.ds(col, 8), :] * keep for i in range(row_block)]
            masked = [x_ref[row + i, here[0], here[1]].astype(F32) * mask[i] for i in range(row_block)]
            acc = [cot_ref[row + i, here[0], here[1]].astype(F32) for i in range(row_block)]
            for b in range(7):
                lines = [pad_ref[tile, row + i, pl.ds(col + 5 + b, 8), 0:width] for i in range(row_block + 6)]
                tap = [
                    jnp.broadcast_to(taps_ref[tile, t : t + 1, 0:width], (8, width))
                    for t in range(48 - b, -1, -7)
                ]
                for i in range(row_block):
                    acc[i] = acc[i] + summed([lines[i + a] * tap[a] for a in range(7)])
                for a in range(7):
                    acc_ref[tile, (6 - a) * 7 + (6 - b), :, 0:width] += summed(
                        [lines[i + a] * masked[i] for i in range(row_block)]
                    )
            for i in range(row_block):
                out_ref[row + i, here[0], here[1]] = acc[i] * mask[i]
            return carry

        lax.fori_loop(0, rows // row_block * strips, block, 0)
    for tile, (start, width) in enumerate(spans):
        taps = jnp.sum(acc_ref[tile], axis=1)[:, 0:width]
        if step:
            taps = taps + refs[1][:, start : start + width]
        tap_grad_ref[:, start : start + width] = taps


def depthwise_back(step, within, grad, rim, x, cot, wet, keep, taps, *before):
    height, across, channels = x.shape
    rows = height // STEPS
    tiles = len(lane_spans(channels))
    part = lambda minor: pl.BlockSpec((rows, across, minor), lambda i: (step, 0, 0))

    def kernel(*refs):
        depthwise_back_kernel(step, *refs)

    return pl.pallas_call(
        kernel,
        grid=(1,),
        out_shape=(jax.ShapeDtypeStruct(x.shape, F32), jax.ShapeDtypeStruct((49, channels), F32)),
        in_specs=[SMEM, VMEM, VMEM, part(channels), part(channels), part(1), VMEM, VMEM]
        + [pl.BlockSpec(memory_space=pl.ANY), VMEM] * (step > 0),
        out_specs=(part(channels), pl.BlockSpec((49, channels), lambda i: (0, 0))),
        scratch_shapes=[
            pltpu.VMEM((tiles, rows + 6, across + 16, 128), F32),
            pltpu.VMEM((tiles, 49, 8, 128), F32),
        ],
        input_output_aliases={8: 0} if step else {},
        compiler_params=pltpu.CompilerParams(vmem_limit_bytes=20 << 20),
        cost_estimate=COST,
        name="depthwise_back_" + "abcd"[step],
    )(within, grad, rim, x, cot, wet, keep, taps, *before)


WIDE, MID, THIN = 128, 64, 8


def packed_rows(cells):
    return cells + cells // 2 + thin_run(cells)


def thin_run(cells):
    return -(-cells // (16 * 8)) * 8


def pieces_of(cells, channels):
    assert channels == WIDE + MID + THIN
    span = lambda first, size: slice(first, first + size)
    half, run = cells // 2, thin_run(cells)
    yield (span(0, cells), span(0, WIDE)), (span(0, cells), span(0, WIDE))
    for side in range(2):
        yield (span(cells, half), span(side * MID, MID)), (span(side * half, half), span(WIDE, MID))
    for group in range(-(-cells // run)):
        size = min(run, cells - group * run)
        yield (
            (span(cells + half, size), span(group * THIN, THIN)),
            (span(group * run, size), span(WIDE + MID, THIN)),
        )


def moved(rows, base):
    return slice(rows.start + base, rows.stop + base)


def pack(packed_ref, index, plain_ref, channels=WIDE + MID + THIN):
    cells = plain_ref.shape[0]
    base = index * packed_rows(cells)
    for (rows, lanes), (cell, channel) in pieces_of(cells, channels):
        packed_ref[moved(rows, base), lanes] = plain_ref[cell, channel].astype(BF16)


def unpack(packed_ref, index, plain_ref, channels=WIDE + MID + THIN):
    cells = plain_ref.shape[0]
    base = index * packed_rows(cells)
    for (rows, lanes), (cell, channel) in pieces_of(cells, channels):
        plain_ref[cell, channel] = packed_ref[moved(rows, base), lanes]


def group_total(row):
    channels = row.shape[1]
    group = lax.broadcasted_iota(jnp.int32, (1, channels), 1) // GROUP_SIZE
    total = jnp.zeros((1, channels), F32)
    for index in range(channels // GROUP_SIZE):
        member = group == index
        total = jnp.where(member, jnp.sum(jnp.where(member, row, 0.0), axis=1, keepdims=True), total)
    return total


def folded(value):
    rows, channels = value.shape
    return jnp.sum(value.reshape(rows // 8, 8, channels), axis=0)


def call(kernel, name, out_shape, specs, scratch=(), limit=12):
    many = isinstance(out_shape, tuple)
    return pl.pallas_call(
        kernel,
        out_shape=out_shape,
        in_specs=specs,
        out_specs=(VMEM,) * len(out_shape) if many else VMEM,
        scratch_shapes=scratch,
        compiler_params=pltpu.CompilerParams(vmem_limit_bytes=limit << 20),
        cost_estimate=COST,
        name=name,
    )


def packed_shape(cells, channels):
    return jax.ShapeDtypeStruct((PARTS * packed_rows(cells // PARTS), WIDE), BF16)


def plain_scratch(cells, channels):
    return pltpu.VMEM((PARTS, cells // PARTS, channels), BF16)


def cut_kernel(cot_ref, wet_ref, packed_ref, bias_ref, plain_ref):
    height, across, channels = cot_ref.shape
    total = jnp.zeros((8, channels), F32)
    for index in range(PARTS):
        rows = height // PARTS

        def one(row, total, index=index, rows=rows):
            grad = (cot_ref[index * rows + row].astype(F32) * wet_ref[index * rows + row]).astype(BF16)
            plain_ref[index, pl.ds(pl.multiple_of(row * across, 8), across), :] = grad
            return total + folded(grad.astype(F32))

        total = lax.fori_loop(0, rows, one, total)
        pack(packed_ref, index, plain_ref.at[index])
    bias_ref[...] = jnp.sum(total, axis=0, keepdims=True)


def cut(cot, wet):
    height, across, channels = cot.shape
    out_shape = (packed_shape(height * across, channels), jax.ShapeDtypeStruct((1, channels), F32))
    scratch = [plain_scratch(height * across, channels)]
    return call(cut_kernel, "cut", out_shape, [VMEM, VMEM], scratch)(cot, wet)


def norm_kernel(*refs):
    conv = refs[:HALVES]
    stat_ref, other_ref, gain_ref, bias_ref, packed_ref, fit_ref, plain_ref = refs[HALVES:]
    rows, across, channels = conv[0].shape
    cells = HALVES * rows * across
    stat, other = stat_ref[...], other_ref[...]
    members = SPAN * GROUP_SIZE
    centre = group_total(stat[0:1] + other[0:1]) / members
    away, other_away = stat[0:1] - centre, other[0:1] - centre
    squares = stat[1:2] + other[1:2] + cells * (away * away + other_away * other_away)
    inverse = lax.rsqrt(group_total(squares) / (members * cells) + EPSILON)
    fit_ref[0:1] = centre
    fit_ref[1:2] = inverse
    gain, bias = gain_ref[...], bias_ref[...]
    for index in range(PARTS):
        half, first = divmod(index * HALVES * rows // PARTS, rows)

        def one(row, carry, index=index, half=half, first=first):
            standard = (conv[half][first + row] - centre) * inverse
            at = pl.multiple_of(row * across, 8)
            plain_ref[index, pl.ds(at, across), :] = (standard * gain + bias).astype(BF16)
            return carry

        lax.fori_loop(0, HALVES * rows // PARTS, one, 0)
        pack(packed_ref, index, plain_ref.at[index])


def norm(conv, stat, other, gain, bias):
    rows, across, channels = conv[0].shape
    cells = HALVES * rows * across
    out_shape = (packed_shape(cells, channels), jax.ShapeDtypeStruct((2, channels), F32))
    size = cells * channels
    scratch = [plain_scratch(cells, channels)]
    return call(norm_kernel, "norm", out_shape, [VMEM] * (4 + HALVES), scratch)(
        *conv, stat, other, gain, bias
    )


def moments_kernel(*refs):
    conv = refs[:HALVES]
    fit_ref, packed_ref, sums_ref, back_ref = refs[HALVES:]
    rows, across, channels = conv[0].shape
    centre, inverse = fit_ref[0:1], fit_ref[1:2]
    sums = (jnp.zeros((8, channels), F32), jnp.zeros((8, channels), F32))
    for index in range(PARTS):
        half, first = divmod(index * HALVES * rows // PARTS, rows)
        unpack(packed_ref, index, back_ref.at[index])

        def one(row, sums, index=index, half=half, first=first):
            standard = (conv[half][first + row] - centre) * inverse
            grad = back_ref[index, pl.ds(pl.multiple_of(row * across, 8), across), :].astype(F32)
            return sums[0] + folded(grad), sums[1] + folded(grad * standard)

        sums = lax.fori_loop(0, HALVES * rows // PARTS, one, sums)
    sums_ref[0:1] = jnp.sum(sums[0], axis=0, keepdims=True)
    sums_ref[1:2] = jnp.sum(sums[1], axis=0, keepdims=True)


def moments(conv, fit, packed):
    rows, across, channels = conv[0].shape
    cells = HALVES * rows * across
    out_shape = (
        jax.ShapeDtypeStruct((2, channels), F32),
        jax.ShapeDtypeStruct((PARTS, cells // PARTS, channels), BF16),
    )
    size = cells * channels
    return call(moments_kernel, "moments", out_shape, [VMEM] * (2 + HALVES))(*conv, fit, packed)


def norm_back_kernel(within_ref, *refs):
    conv = refs[:HALVES]
    fit_ref, back_ref, sums_ref, other_ref, gain_ref, grad_ref, rim_ref, bias_ref = refs[HALVES:]
    rows, across, channels = conv[0].shape
    members = SPAN * GROUP_SIZE * HALVES * rows * across
    centre, inverse = fit_ref[0:1], fit_ref[1:2]
    gain = gain_ref[...]
    sums = sums_ref[...] + other_ref[...]
    mean_first = group_total(sums[0:1] * gain) / members
    mean_second = group_total(sums[1:2] * gain) / members
    total = jnp.zeros((8, channels), F32)
    for index in range(PARTS):
        half, first = divmod(index * HALVES * rows // PARTS, rows)

        def one(row, total, index=index, half=half, first=first):
            standard = (conv[half][first + row] - centre) * inverse
            grad = back_ref[index, pl.ds(pl.multiple_of(row * across, 8), across), :].astype(F32)
            grad = inverse * (grad * gain - mean_first - standard * mean_second)
            grad_ref[half * rows + first + row] = grad
            return total + folded(grad)

        total = lax.fori_loop(0, HALVES * rows // PARTS, one, total)
    bias_ref[...] = jnp.sum(total, axis=0, keepdims=True)
    edge = jnp.where(within_ref[0] == 0, HALVES * rows - 3, 0)
    for index in range(3):
        rim_ref[index] = grad_ref[edge + index].astype(BF16)


def norm_back(within, conv, fit, back, sums, other, gain):
    rows, across, channels = conv[0].shape
    out_shape = (
        jax.ShapeDtypeStruct((HALVES * rows, across, channels), F32),
        jax.ShapeDtypeStruct((3, across, channels), BF16),
        jax.ShapeDtypeStruct((1, channels), F32),
    )
    specs = [SMEM] + [VMEM] * (5 + HALVES)
    return call(norm_back_kernel, "norm_back", out_shape, specs)(
        within, *conv, fit, back, sums, other, gain
    )


def finish_kernel(x_ref, wet_ref, keep_ref, bias_ref, packed_ref, out_ref, plain_ref):
    height, across, channels = x_ref.shape
    keep, bias = keep_ref[...], bias_ref[...]
    rows = height // PARTS
    for index in range(PARTS):
        unpack(packed_ref, index, plain_ref.at[index])

        def one(row, carry, index=index):
            branch = plain_ref[index, pl.ds(pl.multiple_of(row * across, 8), across), :].astype(F32) + bias
            masked = x_ref[index * rows + row].astype(F32) * keep
            out_ref[index * rows + row] = (wet_ref[index * rows + row] * (masked + branch)).astype(BF16)
            return carry

        lax.fori_loop(0, rows, one, 0)


def finish(x, wet, keep, bias, packed):
    height, across, channels = x.shape
    out_shape = jax.ShapeDtypeStruct(x.shape, BF16)
    scratch = [plain_scratch(height * across, channels)]
    return call(finish_kernel, "finish", out_shape, [VMEM] * 5, scratch)(x, wet, keep, bias, packed)


def join_kernel(own_ref, far_ref, sum_ref):
    sum_ref[...] = (own_ref[...].astype(F32) + far_ref[...].astype(F32)).astype(BF16)


def join(own, far):
    out_shape = jax.ShapeDtypeStruct(own.shape, BF16)
    return call(join_kernel, "join", out_shape, [VMEM] * 2)(own, far)


TURNED = (((1,), (1,)), ((), ()))


def piece_shape(part, units):
    full, tail = divmod(units, WIDE)
    rows = 2 * part + 8
    runs = WIDE // tail
    run = -(-rows // (8 * runs)) * 8
    return full, tail, rows, run


def piece_moves(part, units):
    full, tail, rows, run = piece_shape(part, units)
    for kind, first, count in ((0, 0, part), (1, part, part), (2, 2 * part, 8)):
        for tile in range(full):
            lanes = slice(tile * WIDE, (tile + 1) * WIDE)
            at = tile * rows + first
            yield kind, slice(0, count), lanes, slice(at, at + count), slice(0, WIDE)
        row = first
        while row < first + count:
            group = row // run
            stop = min(first + count, (group + 1) * run)
            at = full * rows + row - group * run
            yield (
                kind,
                slice(row - first, stop - first),
                slice(full * WIDE, units),
                slice(at, at + stop - row),
                slice(group * tail, (group + 1) * tail),
            )
            row = stop


def prepare_kernel(in_ref, out_ref, bias_ref, packed_ref, digits_ref):
    part, units = in_ref.shape
    rest = bias_ref[...]
    digits = []
    for _ in range(3):
        digits.append(rest.astype(BF16).astype(F32))
        rest = rest - digits[-1]
    digits_ref[...] = jnp.concatenate(digits + [jnp.zeros((5, units), F32)]).astype(BF16)
    sources = (in_ref, out_ref, digits_ref)
    for kind, rows, lanes, packed_rows_, packed_lanes in piece_moves(part, units):
        packed_ref[packed_rows_, packed_lanes] = sources[kind][rows, lanes]


def prepare(in_rows, out_rows, bias):
    part, units = in_rows.shape
    full, _, rows, run = piece_shape(part, units)
    out_shape = jax.ShapeDtypeStruct((full * rows + run, WIDE), BF16)
    return call(prepare_kernel, "prepare", out_shape, [VMEM] * 3, [pltpu.VMEM((8, units), BF16)])(
        in_rows, out_rows, bias
    )


def spread_weights(pieces, weight_ref, bias_ref, digits_ref, quarter, units, part):
    slot_lanes = weight_ref.shape[2] // 2
    for slot in range(2):
        first = slot * slot_lanes
        for j in range(PARTS):
            piece = pieces[slot * PARTS + j]
            base = pl.multiple_of((quarter ^ j) * LANES, LANES)
            for kind, rows, lanes, packed_rows_, packed_lanes in piece_moves(part, units):
                value = piece[packed_rows_, packed_lanes]
                if kind < 2:
                    at = pl.ds(base + rows.start, rows.stop - rows.start)
                    weight_ref[kind, at, first + lanes.start : first + lanes.stop] = value
                elif j == 0:
                    digits_ref[:, lanes] = value
            for kind in range(2):
                weight_ref[kind, pl.ds(base, part), first + units : first + slot_lanes] = jnp.zeros(
                    (part, slot_lanes - units), BF16
                )
        digits = digits_ref[...].astype(F32)
        bias_ref[0:1, first : first + units] = digits[0:1] + digits[1:2] + digits[2:3]
        bias_ref[0:1, first + units : first + slot_lanes] = jnp.zeros((1, slot_lanes - units), F32)
    for kind in range(2):
        for c in range(PARTS):
            weight_ref[kind, c * LANES + part : (c + 1) * LANES, :] = jnp.zeros((LANES - part, 2 * slot_lanes), BF16)


def spread_cells(packed_ref, plain_ref, turned_ref, channels, filler):
    cells = plain_ref.shape[0]
    for c in range(PARTS):
        view = plain_ref.at[:, c * LANES : (c + 1) * LANES]
        unpack(packed_ref, c, view)
        view[:, channels:LANES] = jnp.zeros((cells, LANES - channels), BF16)
        turned_ref[c, 0:channels, :] = view[:, 0:channels].T
        turned_ref[c, channels : channels + 8, :] = filler


def lane_tiles(lanes):
    return [slice(first, first + TILE) for first in range(0, lanes, TILE)]


def rows_here(cells):
    size = cells // CHUNKS
    step = pl.program_id(0)
    return step // CHUNKS, pl.ds(pl.multiple_of(step % CHUNKS * size, 16), size)


def forward_kernel(units, quarter_ref, *refs):
    packed = refs[:2]
    pieces = refs[2 : 2 + 2 * PARTS]
    own_ref, far_ref, active_ref, slope_ref, turned_out_ref, weight_out_ref = refs[2 + 2 * PARTS : 8 + 2 * PARTS]
    acts_ref, turned_ref, weight_ref, bias_ref, digits_ref, branch_ref, sems = refs[8 + 2 * PARTS :]
    cells = acts_ref.shape[1]
    channels = turned_ref.shape[2] - 8
    outward = [
        pltpu.make_async_copy(weight_ref, weight_out_ref, sems.at[0]),
        pltpu.make_async_copy(turned_ref, turned_out_ref, sems.at[1]),
    ]

    @pl.when(pl.program_id(0) == 0)
    def _():
        spread_weights(pieces, weight_ref, bias_ref, digits_ref, quarter_ref[0], units, channels)
        outward[0].start()
        ones = (lax.broadcasted_iota(jnp.int32, (8, cells), 0) == 0).astype(BF16)
        for side in range(2):
            spread_cells(packed[side], acts_ref.at[side], turned_ref.at[side], channels, ones)
        outward[1].start()

    side, rows = rows_here(cells)
    for tile in lane_tiles(weight_ref.shape[2]):
        value = jnp.dot(acts_ref[side, rows, :], weight_ref[0, :, tile], preferred_element_type=F32)
        value = value + bias_ref[0:1, tile]
        cumulative = 0.5 * (1.0 + lax.erf(value * 0.7071067811865476))
        density = jnp.exp(-0.5 * value * value) * 0.3989422804014327
        active_ref[0, :, tile] = (value * cumulative).astype(BF16)
        slope_ref[0, :, tile] = cumulative + value * density
    branch = lax.dot_general(active_ref[0], weight_ref[1], TURNED, preferred_element_type=F32)
    branch_ref[side, rows, :] = branch.astype(BF16)

    @pl.when(pl.program_id(0) == pl.num_programs(0) - 1)
    def _():
        for side, out_ref in enumerate((own_ref, far_ref)):
            for c in range(PARTS):
                pack(out_ref, c, branch_ref.at[side, :, c * LANES : (c + 1) * LANES])
        for copy in outward:
            copy.wait()


def whole(*shape):
    return pl.BlockSpec(shape, lambda t: (0,) * len(shape), pipeline_mode=pl.Buffered(1))


ANYWHERE = pl.BlockSpec(memory_space=pl.ANY)


def forward(quarter, acts, pieces, units, cells, channels):
    rows = acts[0].shape[0]
    slot_lanes = -(-units // 128) * 128
    lanes = 2 * slot_lanes
    chunk = pl.BlockSpec((1, cells // CHUNKS, lanes), lambda t: (t // CHUNKS, t % CHUNKS, 0))

    def kernel(*refs):
        forward_kernel(units, *refs)

    return pl.pallas_call(
        kernel,
        grid=(2 * CHUNKS,),
        out_shape=(
            jax.ShapeDtypeStruct((rows, WIDE), BF16),
            jax.ShapeDtypeStruct((rows, WIDE), BF16),
            jax.ShapeDtypeStruct((2, cells, lanes), BF16),
            jax.ShapeDtypeStruct((2, cells, lanes), F32),
            jax.ShapeDtypeStruct((2, PARTS, channels + 8, cells), BF16),
            jax.ShapeDtypeStruct((2, PARTS * LANES, lanes), BF16),
        ),
        in_specs=[SMEM] + [whole(rows, WIDE)] * 2 + [whole(*pieces[0].shape)] * (2 * PARTS),
        out_specs=(whole(rows, WIDE),) * 2 + (chunk, chunk, ANYWHERE, ANYWHERE),
        scratch_shapes=[
            pltpu.VMEM((2, cells, PARTS * LANES), BF16),
            pltpu.VMEM((2, PARTS, channels + 8, cells), BF16),
            pltpu.VMEM((2, PARTS * LANES, lanes), BF16),
            pltpu.VMEM((1, lanes), F32),
            pltpu.VMEM((8, units), BF16),
            pltpu.VMEM((2, cells, PARTS * LANES), BF16),
            pltpu.SemaphoreType.DMA((2,)),
        ],
        compiler_params=pltpu.CompilerParams(vmem_limit_bytes=60 << 20, dimension_semantics=("arbitrary",)),
        cost_estimate=COST,
        name="forward",
    )(quarter, *acts, *pieces)


def backward_kernel(*refs):
    packed = refs[:2]
    weight_in_ref, slope_ref, own_ref, far_ref, grad_hidden_ref, turned_out_ref = refs[2:8]
    grads_ref, turned_ref, weight_ref, sems = refs[8:]
    step = pl.program_id(0)
    cells = grads_ref.shape[1]
    lanes = weight_ref.shape[2]
    channels = turned_ref.shape[2] - 8
    inward = pltpu.make_async_copy(weight_in_ref, weight_ref, sems.at[0])
    outward = pltpu.make_async_copy(turned_ref, turned_out_ref, sems.at[1])

    @pl.when(step == 0)
    def _():
        inward.start()
        zeros = jnp.zeros((8, cells), BF16)
        for side in range(2):
            spread_cells(packed[side], grads_ref.at[side], turned_ref.at[side], channels, zeros)
        outward.start()
        inward.wait()

    side, rows = rows_here(cells)
    for tile in lane_tiles(lanes):
        grad = jnp.dot(grads_ref[side, rows, :], weight_ref[1, :, tile], preferred_element_type=F32)
        grad_hidden_ref[0, :, tile] = (grad * slope_ref[0, :, tile]).astype(BF16)
    back = lax.dot_general(grad_hidden_ref[0], weight_ref[0], TURNED, preferred_element_type=F32)
    grads_ref[side, rows, :] = back.astype(BF16)

    @pl.when(step == pl.num_programs(0) - 1)
    def _():
        for side, out_ref in enumerate((own_ref, far_ref)):
            for c in range(PARTS):
                pack(out_ref, c, grads_ref.at[side, :, c * LANES : (c + 1) * LANES])
        outward.wait()


def backward(grads, weights, slope, channels):
    rows = grads[0].shape[0]
    lanes = weights.shape[2]
    cells = slope.shape[1]
    chunk = pl.BlockSpec((1, cells // CHUNKS, lanes), lambda t: (t // CHUNKS, t % CHUNKS, 0))
    return pl.pallas_call(
        backward_kernel,
        grid=(2 * CHUNKS,),
        out_shape=(jax.ShapeDtypeStruct((rows, WIDE), BF16),) * 2
        + (
            jax.ShapeDtypeStruct((2, cells, lanes), BF16),
            jax.ShapeDtypeStruct((2, PARTS, channels + 8, cells), BF16),
        ),
        in_specs=[whole(rows, WIDE)] * 2 + [ANYWHERE, chunk],
        out_specs=(whole(rows, WIDE),) * 2 + (chunk, ANYWHERE),
        scratch_shapes=[
            pltpu.VMEM((2, cells, PARTS * LANES), BF16),
            pltpu.VMEM((2, PARTS, channels + 8, cells), BF16),
            pltpu.VMEM((2, PARTS * LANES, lanes), BF16),
            pltpu.SemaphoreType.DMA((2,)),
        ],
        compiler_params=pltpu.CompilerParams(vmem_limit_bytes=60 << 20, dimension_semantics=("arbitrary",)),
        cost_estimate=COST,
        name="backward",
    )(*grads, weights, slope)


def weight_grads_kernel(quarter_ref, left_ref, right_ref, *refs):
    outs, sum_ref = refs[:PARTS], refs[PARTS]
    _, parts, rows, cells = left_ref.shape
    grad = jnp.dot(left_ref[0].reshape(parts * rows, cells), right_ref[0], preferred_element_type=F32)
    grad = grad + jnp.dot(left_ref[1].reshape(parts * rows, cells), right_ref[1], preferred_element_type=F32)
    sum_ref[...] = grad.reshape(parts, rows, grad.shape[1])
    for j in range(PARTS):
        outs[j][...] = sum_ref[quarter_ref[0] ^ j].astype(outs[j].dtype)


def weight_grads(quarter, left, right, name):
    _, parts, rows, cells = left.shape
    lanes = right.shape[2]
    return pl.pallas_call(
        weight_grads_kernel,
        grid=(lanes // TILE,),
        out_shape=(jax.ShapeDtypeStruct((rows, lanes), F32),) + (jax.ShapeDtypeStruct((rows, lanes), BF16),) * 3,
        in_specs=[SMEM, whole(*left.shape), pl.BlockSpec((2, cells, TILE), lambda t: (0, 0, t))],
        out_specs=(pl.BlockSpec((rows, TILE), lambda t: (0, t)),) * PARTS,
        scratch_shapes=[pltpu.VMEM((parts, rows, TILE), F32)],
        compiler_params=pltpu.CompilerParams(vmem_limit_bytes=60 << 20, dimension_semantics=("arbitrary",)),
        cost_estimate=COST,
        name=name,
    )(quarter, left, right)


def slots_kernel(own_ref, *refs):
    came, (keep_ref, send_ref) = refs[:3], refs[3:]
    lanes = keep_ref.shape[1]
    for first in (0, lanes):
        here = slice(first, first + lanes)
        total = own_ref[:, here]
        for ref in came:
            total = total + ref[:, here].astype(F32)
        if first:
            send_ref[...] = total.astype(BF16)
        else:
            keep_ref[...] = total


def slots(own, *came):
    rows, lanes = own.shape
    out_shape = (jax.ShapeDtypeStruct((rows, lanes // 2), F32), jax.ShapeDtypeStruct((rows, lanes // 2), BF16))
    return call(slots_kernel, "slots", out_shape, [VMEM] * 4)(own, *came)


def add_kernel(keep_ref, came_ref, own_ref, send_ref):
    total = keep_ref[...] + came_ref[...].astype(F32)
    own_ref[...] = total
    send_ref[...] = total.astype(BF16)


def add(keep, came):
    out_shape = (jax.ShapeDtypeStruct(keep.shape, F32), jax.ShapeDtypeStruct(keep.shape, BF16))
    return call(add_kernel, "add", out_shape, [VMEM] * 2)(keep, came)


def gather_kernel(place_ref, *refs):
    near, far = refs[:PARTS], refs[PARTS : 2 * PARTS]
    in_ref, out_ref, bias_ref, held_ref = refs[2 * PARTS :]
    core, quarter = place_ref[0], place_ref[1]
    for j in range(PARTS):
        held_ref[core, quarter ^ j] = near[j][...]
        held_ref[1 - core, quarter ^ j] = far[j][...]
    units = in_ref.shape[1]
    channels = in_ref.shape[0] // PARTS
    for c in range(PARTS):
        in_ref[c * channels : (c + 1) * channels, :] = held_ref[0, c, 0:channels, 0:units].astype(F32)
        out_ref[:, c * channels : (c + 1) * channels] = held_ref[1, c, 0:channels, 0:units].astype(F32).T
    bias_ref[...] = held_ref[0, 0, channels : channels + 8, 0:units].astype(F32)[0:1]


def gather(place, near, far, channels, units):
    rows, lanes = near[0].shape
    return pl.pallas_call(
        gather_kernel,
        out_shape=(
            jax.ShapeDtypeStruct((PARTS * channels, units), F32),
            jax.ShapeDtypeStruct((units, PARTS * channels), F32),
            jax.ShapeDtypeStruct((1, units), F32),
        ),
        in_specs=[SMEM] + [VMEM] * (2 * PARTS),
        out_specs=(VMEM,) * 3,
        scratch_shapes=[pltpu.VMEM((2, PARTS, rows, lanes), BF16)],
        compiler_params=pltpu.CompilerParams(vmem_limit_bytes=16 << 20),
        cost_estimate=COST,
        name="gather",
    )(place, *near, *far)


def after(value, *earlier):
    return lax.optimization_barrier((value, earlier))[0]


def body(
    inputs,
    ocean_mask,
    counts,
    kernel,
    conv_bias,
    norm_gain,
    norm_bias,
    weight_in,
    bias_in,
    weight_out,
    bias_out,
    cotangent,
):
    height, across, channels = inputs.shape
    units = weight_in.shape[1]
    place = lax.axis_index("dp")
    level = lax.axis_index("chan")
    core = place % SPAN
    quarter = place // SPAN % PARTS
    mine = level // 2 == core
    scalar = lambda value: value.astype(jnp.int32).reshape(1)
    row = lambda vector: vector.reshape(1, channels)
    core_of = lambda at: at % SPAN
    owner = lambda at, lev: lev // 2 == core_of(at)
    stranger = lambda at, lev: lev // 2 != core_of(at)
    up_two = lambda at, lev: (at, lev ^ 2)

    piece = prepare(
        lax.dynamic_slice_in_dim(weight_in, quarter * channels, channels, 0),
        lax.dynamic_slice_in_dim(weight_out, quarter * channels, channels, 1).T,
        bias_in.reshape(1, units),
    )
    far_piece = routed(piece, owner, up_two)

    sample = place // SPAN
    count_here = jnp.sum(jnp.where(jnp.arange(counts.shape[0]) == sample, counts, 0))
    channel = level * channels + jnp.arange(channels)
    keep = (channel // (CH // HISTORY) < count_here).astype(F32).reshape(1, channels)
    wet = ocean_mask.astype(F32)[:, :, None]
    edge = jnp.where(core == 0, height - 3, 0)
    outgoing = (
        lax.dynamic_slice_in_dim(inputs, edge, 3, 0).astype(F32) * lax.dynamic_slice_in_dim(wet, edge, 3, 0) * keep
    ).astype(BF16)
    rim = flipped(outgoing, "dp", 1)
    taps = by_lane_tile(kernel.reshape(49, channels))
    bias = by_lane_tile(row(conv_bias))[:, 0]
    upper, upper_stat = depthwise(0, scalar(core), inputs, rim, wet, keep, taps, bias)
    slot = jnp.where(mine, piece, after(far_piece, upper_stat))
    lower, stat = depthwise(1, scalar(core), inputs, rim, wet, keep, taps, bias, after(upper_stat, slot))
    conv = [upper, lower]
    other_slot = flipped(slot, "chan", 1)
    beside, below = flipped(slot, "dp", 2), flipped(slot, "dp", 4)
    stat = after(stat, (other_slot, beside, below))
    normed, fit = norm(conv, stat, flipped(stat, "dp", 1), row(norm_gain), row(norm_bias))
    other_below = flipped(other_slot, "dp", 4)
    grad_branch, grad_bias_out = cut(after(cotangent, normed), wet)
    pieces = [
        slot,
        beside,
        below,
        flipped(after(beside, other_below), "dp", 4),
        other_slot,
        flipped(other_slot, "dp", 2),
        other_below,
        flipped(other_below, "dp", 2),
    ]

    exchanged = lambda cells: lax.all_to_all(cells, "chan", 0, 0, tiled=True)
    other_core = lambda cells: flipped(cells, "dp", 1)
    here = scalar(quarter)
    normed = after(exchanged(normed), (grad_branch, pieces))
    grad_branch = exchanged(after(grad_branch, normed))
    branch_own, branch_far, active, slope, turned, weights = forward(
        here, (normed, other_core(normed)), pieces, units, height // PARTS * across, channels
    )
    straight = lambda sends: [flipped(value, "dp", SPAN * (1 + at)) for at, value in enumerate(sends)]
    beyond = lambda value: routed(value, stranger, up_two)
    branch = join(branch_own, other_core(branch_far))
    grad_branch = after(grad_branch, branch)
    grad_cells = (grad_branch, other_core(grad_branch))
    branch = exchanged(branch)
    back_own, back_far, grad_hidden, turned_grad = backward(grad_cells, weights, slope, channels)
    out_own, *out_sends = weight_grads(here, after(turned_grad, back_own), active, "out_grads")
    back = join(after(back_own, (out_own, branch)), other_core(back_far))
    in_own, *in_sends = weight_grads(here, turned, after(grad_hidden, back), "in_grads")
    out_came = after(straight(out_sends), in_own)
    back = after(exchanged(back), out_came)

    sums, back = moments(after(conv, back), fit, back)
    grad_conv, outgoing_grad, grad_conv_bias = norm_back(
        scalar(core), conv, fit, back, sums, flipped(sums, "dp", 1), row(norm_gain)
    )
    grad_rim = flipped(outgoing_grad, "dp", 1)
    operands = (inputs, cotangent, wet, keep, taps)
    out_slot, out_send = slots(out_own, *after(out_came, grad_conv))
    partial = depthwise_back(0, scalar(core), grad_conv, after(grad_rim, out_send), *operands)
    out_slot, out_send = add(out_slot, after(flipped(out_send, "chan", 1), partial))
    partial = depthwise_back(1, scalar(core), grad_conv, after(grad_rim, out_send), *operands, *partial)
    in_slot, in_send = slots(in_own, *after(straight(in_sends), partial))
    partial = depthwise_back(2, scalar(core), grad_conv, after(grad_rim, in_send), *operands, *partial)
    in_slot, in_send = add(in_slot, after(flipped(in_send, "chan", 1), partial))
    _, out_sum = add(out_slot, after(beyond(out_send), in_send))
    grad_inputs, grad_taps = depthwise_back(
        3, scalar(core), grad_conv, after(grad_rim, (in_send, out_sum)), *operands, *partial
    )
    _, in_sum = add(in_slot, after(beyond(in_send), grad_taps))
    slot_sum = jnp.stack([in_sum, out_sum])
    bit = SPAN * PARTS
    while bit < lax.axis_size("dp"):
        slot_sum = (slot_sum.astype(F32) + flipped(slot_sum, "dp", bit).astype(F32)).astype(BF16)
        bit *= 2
    own_kind = jnp.where(core == 0, slot_sum[0], slot_sum[1])
    other_kind = jnp.where(core == 0, slot_sum[1], slot_sum[0])
    share = jnp.where(mine, own_kind, other_core(other_kind))
    small = jnp.concatenate(
        [grad_taps, grad_conv_bias, sums[1:2], sums[0:1], grad_bias_out, jnp.zeros((3, channels), F32)]
    )
    bit = 1
    while 2 * bit < lax.axis_size("dp"):
        small = small + flipped(small, "dp", bit)
        bit *= 2
    share = after(share, small)
    output = finish(inputs, wet, keep, row(bias_out), after(branch, share))
    shares = after([share] + [flipped(share, "dp", SPAN * j) for j in range(1, PARTS)], output)
    grad_weight_in, grad_weight_out, grad_bias_in = gather(
        jnp.stack([core, quarter]).astype(jnp.int32), shares, [other_core(value) for value in shares], channels, units
    )
    small = small + after(flipped(small, "dp", bit), grad_weight_in)
    return (
        output,
        grad_inputs,
        small[:49].reshape(7, 7, channels),
        small[49],
        small[50],
        small[51],
        grad_weight_in,
        grad_bias_in.reshape(units),
        grad_weight_out,
        small[52],
    )


def solution(mesh):
    in_specs = (
        P("dp", None, "chan"),
        P("dp", None),
        P(),
        P(None, None, "chan"),
        P("chan"),
        P("chan"),
        P("chan"),
        P(None, "chan"),
        P("chan"),
        P("chan", None),
        P("chan"),
        P("dp", None, "chan"),
    )
    out_specs = (
        P("dp", None, "chan"),
        P("dp", None, "chan"),
        P(None, None, "chan"),
        P("chan"),
        P("chan"),
        P("chan"),
        P(None, "chan"),
        P("chan"),
        P("chan", None),
        P("chan"),
    )
    return jax.shard_map(body, mesh=mesh, in_specs=in_specs, out_specs=out_specs, check_vma=False)
```

```python
import jax
import jax.numpy as jnp
from jax import lax
from jax.experimental import pallas as pl
from jax.experimental.pallas import tpu as pltpu
from jax.sharding import PartitionSpec as P

CH = 800
GROUPS = 8
HISTORY = 2
SPAN = 2
EPSILON = 1e-05
GROUP_SIZE = CH // GROUPS
PARTS = 4
HALVES = 2
STEPS = 4
CHUNKS = 3
TILE = 256
COST = pl.CostEstimate(flops=4096, bytes_accessed=4096, transcendentals=0)
LANES = 256
F32 = jnp.float32
BF16 = jnp.bfloat16
VMEM = pl.BlockSpec(memory_space=pltpu.VMEM)
SMEM = pl.BlockSpec(memory_space=pltpu.SMEM)


def flipped(block, axis, bit):
    count = lax.axis_size(axis)
    return lax.ppermute(block, axis, [(place, place ^ bit) for place in range(count)])


def routed(block, allowed, partner):
    count, depth = lax.axis_size("dp"), lax.axis_size("chan")
    route = []
    for place in range(count):
        for level in range(depth):
            if allowed(place, level):
                to_place, to_level = partner(place, level)
                route.append((place * depth + level, to_place * depth + to_level))
    return lax.ppermute(block, ("dp", "chan"), route)


def lane_spans(channels):
    return [(start, min(128, channels - start)) for start in range(0, channels, 128)]


def by_lane_tile(rows):
    count, channels = rows.shape
    tiles = len(lane_spans(channels))
    padded = jnp.pad(rows, ((0, 0), (0, tiles * 128 - channels)))
    return padded.reshape(count, tiles, 128).transpose(1, 0, 2)


def summed(terms):
    while len(terms) > 1:
        terms = [terms[i] + terms[i + 1] for i in range(0, len(terms) - 1, 2)] + terms[len(terms) & ~1 :]
    return terms[0]


def fill_frame(pad_ref, rim_ref, within, first, height, across, spans, load):
    rows = pad_ref.shape[1]

    def store(at, row):
        for tile, (start, width) in enumerate(spans):
            pad_ref[tile, at, 8 : 8 + across, 0:width] = row[:, start : start + width]

    inner = [at for at in range(rows) if 0 <= first - 3 + at < height]

    def fill(at, carry):
        store(at, load(at + first - 3))
        return carry

    lax.fori_loop(inner[0], inner[-1] + 1, fill, 0)
    for at in range(rows):
        source = first - 3 + at
        if source < 0:
            store(at, rim_ref[source + 3].astype(F32) * (within == 1).astype(F32))
        elif source >= height:
            store(at, rim_ref[source - height].astype(F32) * (within == 0).astype(F32))

    def sides(at, carry):
        for tile in range(len(spans)):
            pad_ref[tile, at, 0:8, :] = jnp.zeros((8, 128), F32)
            pad_ref[tile, at, 8 + across : 16 + across, :] = jnp.zeros((8, 128), F32)
        return carry

    lax.fori_loop(0, rows, sides, 0)


def depthwise_kernel(half, within_ref, x_ref, rim_ref, wet_ref, keep_ref, taps_ref, bias_ref, *refs):
    before_ref = refs[0] if half else None
    out_ref, stat_ref, pad_ref, sum_ref = refs[half:]
    height, across, channels = x_ref.shape
    rows = height // HALVES
    row_block = rows
    spans = lane_spans(channels)
    keep = keep_ref[...]
    load = lambda row: x_ref[row].astype(F32) * wet_ref[row] * keep
    fill_frame(pad_ref, rim_ref, within_ref[0], half * rows, height, across, spans, load)
    sum_ref[...] = jnp.zeros_like(sum_ref)
    strips = across // 8
    for tile, (start, width) in enumerate(spans):

        def block(index, carry, tile=tile, start=start, width=width):
            row = index // strips * row_block
            col = pl.multiple_of(index % strips * 8, 8)
            acc = [jnp.broadcast_to(bias_ref[tile : tile + 1, :], (8, 128))] * row_block
            for b in range(7):
                lines = [pad_ref[tile, row + i, pl.ds(col + 5 + b, 8), :] for i in range(row_block + 6)]
                tap = [jnp.broadcast_to(taps_ref[tile, a * 7 + b : a * 7 + b + 1, :], (8, 128)) for a in range(7)]
                for i in range(row_block):
                    acc[i] = acc[i] + summed([lines[i + a] * tap[a] for a in range(7)])
            total = acc[0]
            for i in range(row_block):
                out_ref[row + i, pl.ds(col, 8), start : start + width] = acc[i][:, :width]
                if i:
                    total = total + acc[i]
            sum_ref[tile] += total
            return carry

        lax.fori_loop(0, rows // row_block * strips, block, 0)
    cells = rows * across
    for tile, (start, width) in enumerate(spans):
        mean = jnp.sum(sum_ref[tile], axis=0, keepdims=True)[:, :width] / cells

        def deviations(row, total, start=start, width=width, mean=mean):
            offset = out_ref[row, :, start : start + width] - mean
            return total + jnp.sum((offset * offset).reshape(strips, 8, width), axis=0)

        squares = lax.fori_loop(0, rows, deviations, jnp.zeros((8, width), F32))
        squares = jnp.sum(squares, axis=0, keepdims=True)
        if half:
            other = before_ref[0:1, start : start + width]
            squares = squares + before_ref[1:2, start : start + width] + (mean - other) * (mean - other) * (cells / 2)
            mean = 0.5 * (mean + other)
        stat_ref[0:1, start : start + width] = mean
        stat_ref[1:2, start : start + width] = squares


def depthwise(half, within, x, rim, wet, keep, taps, bias, *before):
    height, across, channels = x.shape
    rows = height // HALVES
    tiles = len(lane_spans(channels))

    def kernel(*refs):
        depthwise_kernel(half, *refs)

    return pl.pallas_call(
        kernel,
        out_shape=(
            jax.ShapeDtypeStruct((rows, across, channels), F32),
            jax.ShapeDtypeStruct((2, channels), F32),
        ),
        in_specs=[SMEM] + [VMEM] * (6 + half),
        out_specs=(VMEM, VMEM),
        scratch_shapes=[
            pltpu.VMEM((tiles, rows + 6, across + 16, 128), F32),
            pltpu.VMEM((tiles, 8, 128), F32),
        ],
        compiler_params=pltpu.CompilerParams(vmem_limit_bytes=16 << 20),
        cost_estimate=COST,
        name="depthwise" + "ab"[half],
    )(within, x, rim, wet, keep, taps, bias, *before)


def depthwise_back_kernel(step, within_ref, grad_ref, rim_ref, x_ref, cot_ref, wet_ref, keep_ref, taps_ref, *refs):
    out_ref, tap_grad_ref, pad_ref, acc_ref = refs[2 * (step > 0) :]
    height, across, channels = grad_ref.shape
    rows = height // STEPS
    row_block = rows
    spans = lane_spans(channels)
    fill_frame(pad_ref, rim_ref, within_ref[0], step * rows, height, across, spans, lambda row: grad_ref[row])
    acc_ref[...] = jnp.zeros_like(acc_ref)
    strips = across // 8
    for tile, (start, width) in enumerate(spans):

        def block(index, carry, tile=tile, start=start, width=width):
            row = index // strips * row_block
            col = pl.multiple_of(index % strips * 8, 8)
            here = (pl.ds(col, 8), slice(start, start + width))
            keep = jnp.broadcast_to(keep_ref[0:1, start : start + width], (8, width))
            mask = [wet_ref[row + i, pl.ds(col, 8), :] * keep for i in range(row_block)]
            masked = [x_ref[row + i, here[0], here[1]].astype(F32) * mask[i] for i in range(row_block)]
            acc = [cot_ref[row + i, here[0], here[1]].astype(F32) for i in range(row_block)]
            for b in range(7):
                lines = [pad_ref[tile, row + i, pl.ds(col + 5 + b, 8), 0:width] for i in range(row_block + 6)]
                tap = [
                    jnp.broadcast_to(taps_ref[tile, t : t + 1, 0:width], (8, width))
                    for t in range(48 - b, -1, -7)
                ]
                for i in range(row_block):
                    acc[i] = acc[i] + summed([lines[i + a] * tap[a] for a in range(7)])
                for a in range(7):
                    acc_ref[tile, (6 - a) * 7 + (6 - b), :, 0:width] += summed(
                        [lines[i + a] * masked[i] for i in range(row_block)]
                    )
            for i in range(row_block):
                out_ref[row + i, here[0], here[1]] = acc[i] * mask[i]
            return carry

        lax.fori_loop(0, rows // row_block * strips, block, 0)
    for tile, (start, width) in enumerate(spans):
        taps = jnp.sum(acc_ref[tile], axis=1)[:, 0:width]
        if step:
            taps = taps + refs[1][:, start : start + width]
        tap_grad_ref[:, start : start + width] = taps


def depthwise_back(step, within, grad, rim, x, cot, wet, keep, taps, *before):
    height, across, channels = x.shape
    rows = height // STEPS
    tiles = len(lane_spans(channels))
    part = lambda minor: pl.BlockSpec((rows, across, minor), lambda i: (step, 0, 0))

    def kernel(*refs):
        depthwise_back_kernel(step, *refs)

    return pl.pallas_call(
        kernel,
        grid=(1,),
        out_shape=(jax.ShapeDtypeStruct(x.shape, F32), jax.ShapeDtypeStruct((49, channels), F32)),
        in_specs=[SMEM, VMEM, VMEM, part(channels), part(channels), part(1), VMEM, VMEM]
        + [pl.BlockSpec(memory_space=pl.ANY), VMEM] * (step > 0),
        out_specs=(part(channels), pl.BlockSpec((49, channels), lambda i: (0, 0))),
        scratch_shapes=[
            pltpu.VMEM((tiles, rows + 6, across + 16, 128), F32),
            pltpu.VMEM((tiles, 49, 8, 128), F32),
        ],
        input_output_aliases={8: 0} if step else {},
        compiler_params=pltpu.CompilerParams(vmem_limit_bytes=20 << 20),
        cost_estimate=COST,
        name="depthwise_back_" + "abcd"[step],
    )(within, grad, rim, x, cot, wet, keep, taps, *before)


WIDE, MID, THIN = 128, 64, 8


def packed_rows(cells):
    return cells + cells // 2 + thin_run(cells)


def thin_run(cells):
    return -(-cells // (16 * 8)) * 8


def pieces_of(cells, channels):
    assert channels == WIDE + MID + THIN
    span = lambda first, size: slice(first, first + size)
    half, run = cells // 2, thin_run(cells)
    yield (span(0, cells), span(0, WIDE)), (span(0, cells), span(0, WIDE))
    for side in range(2):
        yield (span(cells, half), span(side * MID, MID)), (span(side * half, half), span(WIDE, MID))
    for group in range(-(-cells // run)):
        size = min(run, cells - group * run)
        yield (
            (span(cells + half, size), span(group * THIN, THIN)),
            (span(group * run, size), span(WIDE + MID, THIN)),
        )


def moved(rows, base):
    return slice(rows.start + base, rows.stop + base)


def pack(packed_ref, index, plain_ref, channels=WIDE + MID + THIN):
    cells = plain_ref.shape[0]
    base = index * packed_rows(cells)
    for (rows, lanes), (cell, channel) in pieces_of(cells, channels):
        packed_ref[moved(rows, base), lanes] = plain_ref[cell, channel].astype(BF16)


def unpack(packed_ref, index, plain_ref, channels=WIDE + MID + THIN):
    cells = plain_ref.shape[0]
    base = index * packed_rows(cells)
    for (rows, lanes), (cell, channel) in pieces_of(cells, channels):
        plain_ref[cell, channel] = packed_ref[moved(rows, base), lanes]


def group_total(row):
    channels = row.shape[1]
    group = lax.broadcasted_iota(jnp.int32, (1, channels), 1) // GROUP_SIZE
    total = jnp.zeros((1, channels), F32)
    for index in range(channels // GROUP_SIZE):
        member = group == index
        total = jnp.where(member, jnp.sum(jnp.where(member, row, 0.0), axis=1, keepdims=True), total)
    return total


def folded(value):
    rows, channels = value.shape
    return jnp.sum(value.reshape(rows // 8, 8, channels), axis=0)


def call(kernel, name, out_shape, specs, scratch=(), limit=12):
    many = isinstance(out_shape, tuple)
    return pl.pallas_call(
        kernel,
        out_shape=out_shape,
        in_specs=specs,
        out_specs=(VMEM,) * len(out_shape) if many else VMEM,
        scratch_shapes=scratch,
        compiler_params=pltpu.CompilerParams(vmem_limit_bytes=limit << 20),
        cost_estimate=COST,
        name=name,
    )


def packed_shape(cells, channels):
    return jax.ShapeDtypeStruct((PARTS * packed_rows(cells // PARTS), WIDE), BF16)


def plain_scratch(cells, channels):
    return pltpu.VMEM((PARTS, cells // PARTS, channels), BF16)


def cut_kernel(cot_ref, wet_ref, packed_ref, bias_ref, plain_ref):
    height, across, channels = cot_ref.shape
    total = jnp.zeros((8, channels), F32)
    for index in range(PARTS):
        rows = height // PARTS

        def one(row, total, index=index, rows=rows):
            grad = (cot_ref[index * rows + row].astype(F32) * wet_ref[index * rows + row]).astype(BF16)
            plain_ref[index, pl.ds(pl.multiple_of(row * across, 8), across), :] = grad
            return total + folded(grad.astype(F32))

        total = lax.fori_loop(0, rows, one, total)
        pack(packed_ref, index, plain_ref.at[index])
    bias_ref[...] = jnp.sum(total, axis=0, keepdims=True)


def cut(cot, wet):
    height, across, channels = cot.shape
    out_shape = (packed_shape(height * across, channels), jax.ShapeDtypeStruct((1, channels), F32))
    scratch = [plain_scratch(height * across, channels)]
    return call(cut_kernel, "cut", out_shape, [VMEM, VMEM], scratch)(cot, wet)


def norm_kernel(*refs):
    conv = refs[:HALVES]
    stat_ref, other_ref, gain_ref, bias_ref, packed_ref, fit_ref, plain_ref = refs[HALVES:]
    rows, across, channels = conv[0].shape
    cells = HALVES * rows * across
    stat, other = stat_ref[...], other_ref[...]
    members = SPAN * GROUP_SIZE
    centre = group_total(stat[0:1] + other[0:1]) / members
    away, other_away = stat[0:1] - centre, other[0:1] - centre
    squares = stat[1:2] + other[1:2] + cells * (away * away + other_away * other_away)
    inverse = lax.rsqrt(group_total(squares) / (members * cells) + EPSILON)
    fit_ref[0:1] = centre
    fit_ref[1:2] = inverse
    gain, bias = gain_ref[...], bias_ref[...]
    for index in range(PARTS):
        half, first = divmod(index * HALVES * rows // PARTS, rows)

        def one(row, carry, index=index, half=half, first=first):
            standard = (conv[half][first + row] - centre) * inverse
            at = pl.multiple_of(row * across, 8)
            plain_ref[index, pl.ds(at, across), :] = (standard * gain + bias).astype(BF16)
            return carry

        lax.fori_loop(0, HALVES * rows // PARTS, one, 0)
        pack(packed_ref, index, plain_ref.at[index])


def norm(conv, stat, other, gain, bias):
    rows, across, channels = conv[0].shape
    cells = HALVES * rows * across
    out_shape = (packed_shape(cells, channels), jax.ShapeDtypeStruct((2, channels), F32))
    size = cells * channels
    scratch = [plain_scratch(cells, channels)]
    return call(norm_kernel, "norm", out_shape, [VMEM] * (4 + HALVES), scratch)(
        *conv, stat, other, gain, bias
    )


def moments_kernel(*refs):
    conv = refs[:HALVES]
    fit_ref, packed_ref, sums_ref, back_ref = refs[HALVES:]
    rows, across, channels = conv[0].shape
    centre, inverse = fit_ref[0:1], fit_ref[1:2]
    sums = (jnp.zeros((8, channels), F32), jnp.zeros((8, channels), F32))
    for index in range(PARTS):
        half, first = divmod(index * HALVES * rows // PARTS, rows)
        unpack(packed_ref, index, back_ref.at[index])

        def one(row, sums, index=index, half=half, first=first):
            standard = (conv[half][first + row] - centre) * inverse
            grad = back_ref[index, pl.ds(pl.multiple_of(row * across, 8), across), :].astype(F32)
            return sums[0] + folded(grad), sums[1] + folded(grad * standard)

        sums = lax.fori_loop(0, HALVES * rows // PARTS, one, sums)
    sums_ref[0:1] = jnp.sum(sums[0], axis=0, keepdims=True)
    sums_ref[1:2] = jnp.sum(sums[1], axis=0, keepdims=True)


def moments(conv, fit, packed):
    rows, across, channels = conv[0].shape
    cells = HALVES * rows * across
    out_shape = (
        jax.ShapeDtypeStruct((2, channels), F32),
        jax.ShapeDtypeStruct((PARTS, cells // PARTS, channels), BF16),
    )
    size = cells * channels
    return call(moments_kernel, "moments", out_shape, [VMEM] * (2 + HALVES))(*conv, fit, packed)


def norm_back_kernel(within_ref, *refs):
    conv = refs[:HALVES]
    fit_ref, back_ref, sums_ref, other_ref, gain_ref, grad_ref, rim_ref, bias_ref = refs[HALVES:]
    rows, across, channels = conv[0].shape
    members = SPAN * GROUP_SIZE * HALVES * rows * across
    centre, inverse = fit_ref[0:1], fit_ref[1:2]
    gain = gain_ref[...]
    sums = sums_ref[...] + other_ref[...]
    mean_first = group_total(sums[0:1] * gain) / members
    mean_second = group_total(sums[1:2] * gain) / members
    total = jnp.zeros((8, channels), F32)
    for index in range(PARTS):
        half, first = divmod(index * HALVES * rows // PARTS, rows)

        def one(row, total, index=index, half=half, first=first):
            standard = (conv[half][first + row] - centre) * inverse
            grad = back_ref[index, pl.ds(pl.multiple_of(row * across, 8), across), :].astype(F32)
            grad = inverse * (grad * gain - mean_first - standard * mean_second)
            grad_ref[half * rows + first + row] = grad
            return total + folded(grad)

        total = lax.fori_loop(0, HALVES * rows // PARTS, one, total)
    bias_ref[...] = jnp.sum(total, axis=0, keepdims=True)
    edge = jnp.where(within_ref[0] == 0, HALVES * rows - 3, 0)
    for index in range(3):
        rim_ref[index] = grad_ref[edge + index].astype(BF16)


def norm_back(within, conv, fit, back, sums, other, gain):
    rows, across, channels = conv[0].shape
    out_shape = (
        jax.ShapeDtypeStruct((HALVES * rows, across, channels), F32),
        jax.ShapeDtypeStruct((3, across, channels), BF16),
        jax.ShapeDtypeStruct((1, channels), F32),
    )
    specs = [SMEM] + [VMEM] * (5 + HALVES)
    return call(norm_back_kernel, "norm_back", out_shape, specs)(
        within, *conv, fit, back, sums, other, gain
    )


def finish_kernel(x_ref, wet_ref, keep_ref, bias_ref, packed_ref, out_ref, plain_ref):
    height, across, channels = x_ref.shape
    keep, bias = keep_ref[...], bias_ref[...]
    rows = height // PARTS
    for index in range(PARTS):
        unpack(packed_ref, index, plain_ref.at[index])

        def one(row, carry, index=index):
            branch = plain_ref[index, pl.ds(pl.multiple_of(row * across, 8), across), :].astype(F32) + bias
            masked = x_ref[index * rows + row].astype(F32) * keep
            out_ref[index * rows + row] = (wet_ref[index * rows + row] * (masked + branch)).astype(BF16)
            return carry

        lax.fori_loop(0, rows, one, 0)


def finish(x, wet, keep, bias, packed):
    height, across, channels = x.shape
    out_shape = jax.ShapeDtypeStruct(x.shape, BF16)
    scratch = [plain_scratch(height * across, channels)]
    return call(finish_kernel, "finish", out_shape, [VMEM] * 5, scratch)(x, wet, keep, bias, packed)


def join_kernel(own_ref, far_ref, sum_ref):
    sum_ref[...] = (own_ref[...].astype(F32) + far_ref[...].astype(F32)).astype(BF16)


def join(own, far):
    out_shape = jax.ShapeDtypeStruct(own.shape, BF16)
    return call(join_kernel, "join", out_shape, [VMEM] * 2)(own, far)


TURNED = (((1,), (1,)), ((), ()))


def piece_shape(part, units):
    full, tail = divmod(units, WIDE)
    rows = 2 * part + 8
    runs = WIDE // tail
    run = -(-rows // (8 * runs)) * 8
    return full, tail, rows, run


def piece_moves(part, units):
    full, tail, rows, run = piece_shape(part, units)
    for kind, first, count in ((0, 0, part), (1, part, part), (2, 2 * part, 8)):
        for tile in range(full):
            lanes = slice(tile * WIDE, (tile + 1) * WIDE)
            at = tile * rows + first
            yield kind, slice(0, count), lanes, slice(at, at + count), slice(0, WIDE)
        row = first
        while row < first + count:
            group = row // run
            stop = min(first + count, (group + 1) * run)
            at = full * rows + row - group * run
            yield (
                kind,
                slice(row - first, stop - first),
                slice(full * WIDE, units),
                slice(at, at + stop - row),
                slice(group * tail, (group + 1) * tail),
            )
            row = stop


def prepare_kernel(in_ref, out_ref, bias_ref, packed_ref, digits_ref):
    part, units = in_ref.shape
    rest = bias_ref[...]
    digits = []
    for _ in range(3):
        digits.append(rest.astype(BF16).astype(F32))
        rest = rest - digits[-1]
    digits_ref[...] = jnp.concatenate(digits + [jnp.zeros((5, units), F32)]).astype(BF16)
    sources = (in_ref, out_ref, digits_ref)
    for kind, rows, lanes, packed_rows_, packed_lanes in piece_moves(part, units):
        packed_ref[packed_rows_, packed_lanes] = sources[kind][rows, lanes]


def prepare(in_rows, out_rows, bias):
    part, units = in_rows.shape
    full, _, rows, run = piece_shape(part, units)
    out_shape = jax.ShapeDtypeStruct((full * rows + run, WIDE), BF16)
    return call(prepare_kernel, "prepare", out_shape, [VMEM] * 3, [pltpu.VMEM((8, units), BF16)])(
        in_rows, out_rows, bias
    )


def spread_weights(pieces, weight_ref, bias_ref, digits_ref, quarter, units, part):
    slot_lanes = weight_ref.shape[2] // 2
    for slot in range(2):
        first = slot * slot_lanes
        for j in range(PARTS):
            piece = pieces[slot * PARTS + j]
            base = pl.multiple_of((quarter ^ j) * LANES, LANES)
            for kind, rows, lanes, packed_rows_, packed_lanes in piece_moves(part, units):
                value = piece[packed_rows_, packed_lanes]
                if kind < 2:
                    at = pl.ds(base + rows.start, rows.stop - rows.start)
                    weight_ref[kind, at, first + lanes.start : first + lanes.stop] = value
                elif j == 0:
                    digits_ref[:, lanes] = value
            for kind in range(2):
                weight_ref[kind, pl.ds(base, part), first + units : first + slot_lanes] = jnp.zeros(
                    (part, slot_lanes - units), BF16
                )
        digits = digits_ref[...].astype(F32)
        bias_ref[0:1, first : first + units] = digits[0:1] + digits[1:2] + digits[2:3]
        bias_ref[0:1, first + units : first + slot_lanes] = jnp.zeros((1, slot_lanes - units), F32)
    for kind in range(2):
        for c in range(PARTS):
            weight_ref[kind, c * LANES + part : (c + 1) * LANES, :] = jnp.zeros((LANES - part, 2 * slot_lanes), BF16)


def spread_cells(packed_ref, plain_ref, turned_ref, channels, filler):
    cells = plain_ref.shape[0]
    for c in range(PARTS):
        view = plain_ref.at[:, c * LANES : (c + 1) * LANES]
        unpack(packed_ref, c, view)
        view[:, channels:LANES] = jnp.zeros((cells, LANES - channels), BF16)
        turned_ref[c, 0:channels, :] = view[:, 0:channels].T
        turned_ref[c, channels : channels + 8, :] = filler


def lane_tiles(lanes):
    return [slice(first, first + TILE) for first in range(0, lanes, TILE)]


def rows_here(cells):
    size = cells // CHUNKS
    step = pl.program_id(0)
    return step // CHUNKS, pl.ds(pl.multiple_of(step % CHUNKS * size, 16), size)


def forward_kernel(units, quarter_ref, *refs):
    packed = refs[:2]
    pieces = refs[2 : 2 + 2 * PARTS]
    own_ref, far_ref, active_ref, slope_ref, turned_out_ref, weight_out_ref = refs[2 + 2 * PARTS : 8 + 2 * PARTS]
    acts_ref, turned_ref, weight_ref, bias_ref, digits_ref, branch_ref, sems = refs[8 + 2 * PARTS :]
    cells = acts_ref.shape[1]
    channels = turned_ref.shape[2] - 8
    outward = [
        pltpu.make_async_copy(weight_ref, weight_out_ref, sems.at[0]),
        pltpu.make_async_copy(turned_ref, turned_out_ref, sems.at[1]),
    ]

    @pl.when(pl.program_id(0) == 0)
    def _():
        spread_weights(pieces, weight_ref, bias_ref, digits_ref, quarter_ref[0], units, channels)
        outward[0].start()
        ones = (lax.broadcasted_iota(jnp.int32, (8, cells), 0) == 0).astype(BF16)
        for side in range(2):
            spread_cells(packed[side], acts_ref.at[side], turned_ref.at[side], channels, ones)
        outward[1].start()

    side, rows = rows_here(cells)
    for tile in lane_tiles(weight_ref.shape[2]):
        value = jnp.dot(acts_ref[side, rows, :], weight_ref[0, :, tile], preferred_element_type=F32)
        value = value + bias_ref[0:1, tile]
        cumulative = 0.5 * (1.0 + lax.erf(value * 0.7071067811865476))
        density = jnp.exp(-0.5 * value * value) * 0.3989422804014327
        active_ref[0, :, tile] = (value * cumulative).astype(BF16)
        slope_ref[0, :, tile] = cumulative + value * density
    branch = lax.dot_general(active_ref[0], weight_ref[1], TURNED, preferred_element_type=F32)
    branch_ref[side, rows, :] = branch.astype(BF16)

    @pl.when(pl.program_id(0) == pl.num_programs(0) - 1)
    def _():
        for side, out_ref in enumerate((own_ref, far_ref)):
            for c in range(PARTS):
                pack(out_ref, c, branch_ref.at[side, :, c * LANES : (c + 1) * LANES])
        for copy in outward:
            copy.wait()


def whole(*shape):
    return pl.BlockSpec(shape, lambda t: (0,) * len(shape), pipeline_mode=pl.Buffered(1))


ANYWHERE = pl.BlockSpec(memory_space=pl.ANY)


def forward(quarter, acts, pieces, units, cells, channels):
    rows = acts[0].shape[0]
    slot_lanes = -(-units // 128) * 128
    lanes = 2 * slot_lanes
    chunk = pl.BlockSpec((1, cells // CHUNKS, lanes), lambda t: (t // CHUNKS, t % CHUNKS, 0))

    def kernel(*refs):
        forward_kernel(units, *refs)

    return pl.pallas_call(
        kernel,
        grid=(2 * CHUNKS,),
        out_shape=(
            jax.ShapeDtypeStruct((rows, WIDE), BF16),
            jax.ShapeDtypeStruct((rows, WIDE), BF16),
            jax.ShapeDtypeStruct((2, cells, lanes), BF16),
            jax.ShapeDtypeStruct((2, cells, lanes), F32),
            jax.ShapeDtypeStruct((2, PARTS, channels + 8, cells), BF16),
            jax.ShapeDtypeStruct((2, PARTS * LANES, lanes), BF16),
        ),
        in_specs=[SMEM] + [whole(rows, WIDE)] * 2 + [whole(*pieces[0].shape)] * (2 * PARTS),
        out_specs=(whole(rows, WIDE),) * 2 + (chunk, chunk, ANYWHERE, ANYWHERE),
        scratch_shapes=[
            pltpu.VMEM((2, cells, PARTS * LANES), BF16),
            pltpu.VMEM((2, PARTS, channels + 8, cells), BF16),
            pltpu.VMEM((2, PARTS * LANES, lanes), BF16),
            pltpu.VMEM((1, lanes), F32),
            pltpu.VMEM((8, units), BF16),
            pltpu.VMEM((2, cells, PARTS * LANES), BF16),
            pltpu.SemaphoreType.DMA((2,)),
        ],
        compiler_params=pltpu.CompilerParams(vmem_limit_bytes=60 << 20, dimension_semantics=("arbitrary",)),
        cost_estimate=COST,
        name="forward",
    )(quarter, *acts, *pieces)


def backward_kernel(*refs):
    packed = refs[:2]
    weight_in_ref, slope_ref, own_ref, far_ref, grad_hidden_ref, turned_out_ref = refs[2:8]
    grads_ref, turned_ref, weight_ref, sems = refs[8:]
    step = pl.program_id(0)
    cells = grads_ref.shape[1]
    lanes = weight_ref.shape[2]
    channels = turned_ref.shape[2] - 8
    inward = pltpu.make_async_copy(weight_in_ref, weight_ref, sems.at[0])
    outward = pltpu.make_async_copy(turned_ref, turned_out_ref, sems.at[1])

    @pl.when(step == 0)
    def _():
        inward.start()
        zeros = jnp.zeros((8, cells), BF16)
        for side in range(2):
            spread_cells(packed[side], grads_ref.at[side], turned_ref.at[side], channels, zeros)
        outward.start()
        inward.wait()

    side, rows = rows_here(cells)
    for tile in lane_tiles(lanes):
        grad = jnp.dot(grads_ref[side, rows, :], weight_ref[1, :, tile], preferred_element_type=F32)
        grad_hidden_ref[0, :, tile] = (grad * slope_ref[0, :, tile]).astype(BF16)
    back = lax.dot_general(grad_hidden_ref[0], weight_ref[0], TURNED, preferred_element_type=F32)
    grads_ref[side, rows, :] = back.astype(BF16)

    @pl.when(step == pl.num_programs(0) - 1)
    def _():
        for side, out_ref in enumerate((own_ref, far_ref)):
            for c in range(PARTS):
                pack(out_ref, c, grads_ref.at[side, :, c * LANES : (c + 1) * LANES])
        outward.wait()


def backward(grads, weights, slope, channels):
    rows = grads[0].shape[0]
    lanes = weights.shape[2]
    cells = slope.shape[1]
    chunk = pl.BlockSpec((1, cells // CHUNKS, lanes), lambda t: (t // CHUNKS, t % CHUNKS, 0))
    return pl.pallas_call(
        backward_kernel,
        grid=(2 * CHUNKS,),
        out_shape=(jax.ShapeDtypeStruct((rows, WIDE), BF16),) * 2
        + (
            jax.ShapeDtypeStruct((2, cells, lanes), BF16),
            jax.ShapeDtypeStruct((2, PARTS, channels + 8, cells), BF16),
        ),
        in_specs=[whole(rows, WIDE)] * 2 + [ANYWHERE, chunk],
        out_specs=(whole(rows, WIDE),) * 2 + (chunk, ANYWHERE),
        scratch_shapes=[
            pltpu.VMEM((2, cells, PARTS * LANES), BF16),
            pltpu.VMEM((2, PARTS, channels + 8, cells), BF16),
            pltpu.VMEM((2, PARTS * LANES, lanes), BF16),
            pltpu.SemaphoreType.DMA((2,)),
        ],
        compiler_params=pltpu.CompilerParams(vmem_limit_bytes=60 << 20, dimension_semantics=("arbitrary",)),
        cost_estimate=COST,
        name="backward",
    )(*grads, weights, slope)


def weight_grads_kernel(quarter_ref, left_ref, right_ref, *refs):
    outs, sum_ref = refs[:PARTS], refs[PARTS]
    _, parts, rows, cells = left_ref.shape
    grad = jnp.dot(left_ref[0].reshape(parts * rows, cells), right_ref[0], preferred_element_type=F32)
    grad = grad + jnp.dot(left_ref[1].reshape(parts * rows, cells), right_ref[1], preferred_element_type=F32)
    sum_ref[...] = grad.reshape(parts, rows, grad.shape[1])
    for j in range(PARTS):
        outs[j][...] = sum_ref[quarter_ref[0] ^ j].astype(outs[j].dtype)


def weight_grads(quarter, left, right, name):
    _, parts, rows, cells = left.shape
    lanes = right.shape[2]
    return pl.pallas_call(
        weight_grads_kernel,
        grid=(lanes // TILE,),
        out_shape=(jax.ShapeDtypeStruct((rows, lanes), F32),) + (jax.ShapeDtypeStruct((rows, lanes), BF16),) * 3,
        in_specs=[SMEM, whole(*left.shape), pl.BlockSpec((2, cells, TILE), lambda t: (0, 0, t))],
        out_specs=(pl.BlockSpec((rows, TILE), lambda t: (0, t)),) * PARTS,
        scratch_shapes=[pltpu.VMEM((parts, rows, TILE), F32)],
        compiler_params=pltpu.CompilerParams(vmem_limit_bytes=60 << 20, dimension_semantics=("arbitrary",)),
        cost_estimate=COST,
        name=name,
    )(quarter, left, right)


def slots_kernel(own_ref, *refs):
    came, (keep_ref, send_ref) = refs[:3], refs[3:]
    lanes = keep_ref.shape[1]
    for first in (0, lanes):
        here = slice(first, first + lanes)
        total = own_ref[:, here]
        for ref in came:
            total = total + ref[:, here].astype(F32)
        if first:
            send_ref[...] = total.astype(BF16)
        else:
            keep_ref[...] = total


def slots(own, *came):
    rows, lanes = own.shape
    out_shape = (jax.ShapeDtypeStruct((rows, lanes // 2), F32), jax.ShapeDtypeStruct((rows, lanes // 2), BF16))
    return call(slots_kernel, "slots", out_shape, [VMEM] * 4)(own, *came)


def add_kernel(keep_ref, came_ref, own_ref, send_ref):
    total = keep_ref[...] + came_ref[...].astype(F32)
    own_ref[...] = total
    send_ref[...] = total.astype(BF16)


def add(keep, came):
    out_shape = (jax.ShapeDtypeStruct(keep.shape, F32), jax.ShapeDtypeStruct(keep.shape, BF16))
    return call(add_kernel, "add", out_shape, [VMEM] * 2)(keep, came)


def gather_kernel(place_ref, *refs):
    near, far = refs[:PARTS], refs[PARTS : 2 * PARTS]
    in_ref, out_ref, bias_ref, held_ref = refs[2 * PARTS :]
    core, quarter = place_ref[0], place_ref[1]
    for j in range(PARTS):
        held_ref[core, quarter ^ j] = near[j][...]
        held_ref[1 - core, quarter ^ j] = far[j][...]
    units = in_ref.shape[1]
    channels = in_ref.shape[0] // PARTS
    for c in range(PARTS):
        in_ref[c * channels : (c + 1) * channels, :] = held_ref[0, c, 0:channels, 0:units].astype(F32)
        out_ref[:, c * channels : (c + 1) * channels] = held_ref[1, c, 0:channels, 0:units].astype(F32).T
    bias_ref[...] = held_ref[0, 0, channels : channels + 8, 0:units].astype(F32)[0:1]


def gather(place, near, far, channels, units):
    rows, lanes = near[0].shape
    return pl.pallas_call(
        gather_kernel,
        out_shape=(
            jax.ShapeDtypeStruct((PARTS * channels, units), F32),
            jax.ShapeDtypeStruct((units, PARTS * channels), F32),
            jax.ShapeDtypeStruct((1, units), F32),
        ),
        in_specs=[SMEM] + [VMEM] * (2 * PARTS),
        out_specs=(VMEM,) * 3,
        scratch_shapes=[pltpu.VMEM((2, PARTS, rows, lanes), BF16)],
        compiler_params=pltpu.CompilerParams(vmem_limit_bytes=16 << 20),
        cost_estimate=COST,
        name="gather",
    )(place, *near, *far)


def after(value, *earlier):
    return lax.optimization_barrier((value, earlier))[0]


def body(
    inputs,
    ocean_mask,
    counts,
    kernel,
    conv_bias,
    norm_gain,
    norm_bias,
    weight_in,
    bias_in,
    weight_out,
    bias_out,
    cotangent,
):
    height, across, channels = inputs.shape
    units = weight_in.shape[1]
    place = lax.axis_index("dp")
    level = lax.axis_index("chan")
    core = place % SPAN
    quarter = place // SPAN % PARTS
    mine = level // 2 == core
    scalar = lambda value: value.astype(jnp.int32).reshape(1)
    row = lambda vector: vector.reshape(1, channels)
    core_of = lambda at: at % SPAN
    owner = lambda at, lev: lev // 2 == core_of(at)
    stranger = lambda at, lev: lev // 2 != core_of(at)
    up_two = lambda at, lev: (at, lev ^ 2)

    piece = prepare(
        lax.dynamic_slice_in_dim(weight_in, quarter * channels, channels, 0),
        lax.dynamic_slice_in_dim(weight_out, quarter * channels, channels, 1).T,
        bias_in.reshape(1, units),
    )
    far_piece = routed(piece, owner, up_two)

    sample = place // SPAN
    count_here = jnp.sum(jnp.where(jnp.arange(counts.shape[0]) == sample, counts, 0))
    channel = level * channels + jnp.arange(channels)
    keep = (channel // (CH // HISTORY) < count_here).astype(F32).reshape(1, channels)
    wet = ocean_mask.astype(F32)[:, :, None]
    edge = jnp.where(core == 0, height - 3, 0)
    outgoing = (
        lax.dynamic_slice_in_dim(inputs, edge, 3, 0).astype(F32) * lax.dynamic_slice_in_dim(wet, edge, 3, 0) * keep
    ).astype(BF16)
    rim = flipped(outgoing, "dp", 1)
    taps = by_lane_tile(kernel.reshape(49, channels))
    bias = by_lane_tile(row(conv_bias))[:, 0]
    upper, upper_stat = depthwise(0, scalar(core), inputs, rim, wet, keep, taps, bias)
    slot = jnp.where(mine, piece, after(far_piece, upper_stat))
    lower, stat = depthwise(1, scalar(core), inputs, rim, wet, keep, taps, bias, after(upper_stat, slot))
    conv = [upper, lower]
    other_slot = flipped(slot, "chan", 1)
    beside, below = flipped(slot, "dp", 2), flipped(slot, "dp", 4)
    stat = after(stat, (other_slot, beside, below))
    normed, fit = norm(conv, stat, flipped(stat, "dp", 1), row(norm_gain), row(norm_bias))
    other_below = flipped(other_slot, "dp", 4)
    grad_branch, grad_bias_out = cut(after(cotangent, normed), wet)
    pieces = [
        slot,
        beside,
        below,
        flipped(after(beside, other_below), "dp", 4),
        other_slot,
        flipped(other_slot, "dp", 2),
        other_below,
        flipped(other_below, "dp", 2),
    ]

    exchanged = lambda cells: lax.all_to_all(cells, "chan", 0, 0, tiled=True)
    other_core = lambda cells: flipped(cells, "dp", 1)
    here = scalar(quarter)
    normed = after(exchanged(normed), (grad_branch, pieces))
    grad_branch = exchanged(after(grad_branch, normed))
    branch_own, branch_far, active, slope, turned, weights = forward(
        here, (normed, other_core(normed)), pieces, units, height // PARTS * across, channels
    )
    straight = lambda sends: [flipped(value, "dp", SPAN * (1 + at)) for at, value in enumerate(sends)]
    beyond = lambda value: routed(value, stranger, up_two)
    branch = join(branch_own, other_core(branch_far))
    grad_branch = after(grad_branch, branch)
    grad_cells = (grad_branch, other_core(grad_branch))
    branch = exchanged(branch)
    back_own, back_far, grad_hidden, turned_grad = backward(grad_cells, weights, slope, channels)
    out_own, *out_sends = weight_grads(here, after(turned_grad, back_own), active, "out_grads")
    back = join(after(back_own, (out_own, branch)), other_core(back_far))
    in_own, *in_sends = weight_grads(here, turned, after(grad_hidden, back), "in_grads")
    out_came = after(straight(out_sends), in_own)
    back = after(exchanged(back), out_came)

    sums, back = moments(after(conv, back), fit, back)
    grad_conv, outgoing_grad, grad_conv_bias = norm_back(
        scalar(core), conv, fit, back, sums, flipped(sums, "dp", 1), row(norm_gain)
    )
    grad_rim = flipped(outgoing_grad, "dp", 1)
    operands = (inputs, cotangent, wet, keep, taps)
    out_slot, out_send = slots(out_own, *after(out_came, grad_conv))
    partial = depthwise_back(0, scalar(core), grad_conv, after(grad_rim, out_send), *operands)
    out_slot, out_send = add(out_slot, after(flipped(out_send, "chan", 1), partial))
    partial = depthwise_back(1, scalar(core), grad_conv, after(grad_rim, out_send), *operands, *partial)
    in_slot, in_send = slots(in_own, *after(straight(in_sends), partial))
    partial = depthwise_back(2, scalar(core), grad_conv, after(grad_rim, in_send), *operands, *partial)
    in_slot, in_send = add(in_slot, after(flipped(in_send, "chan", 1), partial))
    _, out_sum = add(out_slot, after(beyond(out_send), in_send))
    grad_inputs, grad_taps = depthwise_back(
        3, scalar(core), grad_conv, after(grad_rim, (in_send, out_sum)), *operands, *partial
    )
    _, in_sum = add(in_slot, after(beyond(in_send), grad_taps))
    slot_sum = jnp.stack([in_sum, out_sum])
    bit = SPAN * PARTS
    while bit < lax.axis_size("dp"):
        slot_sum = (slot_sum.astype(F32) + flipped(slot_sum, "dp", bit).astype(F32)).astype(BF16)
        bit *= 2
    own_kind = jnp.where(core == 0, slot_sum[0], slot_sum[1])
    other_kind = jnp.where(core == 0, slot_sum[1], slot_sum[0])
    share = jnp.where(mine, own_kind, other_core(other_kind))
    small = jnp.concatenate(
        [grad_taps, grad_conv_bias, sums[1:2], sums[0:1], grad_bias_out, jnp.zeros((3, channels), F32)]
    )
    bit = 1
    output = finish(inputs, wet, keep, row(bias_out), after(branch, share))
    while 2 * bit < lax.axis_size("dp"):
        small = small + (after(flipped(small, "dp", bit), output) if bit > 1 else flipped(small, "dp", bit))
        bit *= 2
    shares = after([share] + [flipped(share, "dp", SPAN * j) for j in range(1, PARTS)], (output, small))
    grad_weight_in, grad_weight_out, grad_bias_in = gather(
        jnp.stack([core, quarter]).astype(jnp.int32), shares, [other_core(value) for value in shares], channels, units
    )
    small = small + after(flipped(small, "dp", bit), grad_weight_in)
    return (
        output,
        grad_inputs,
        small[:49].reshape(7, 7, channels),
        small[49],
        small[50],
        small[51],
        grad_weight_in,
        grad_bias_in.reshape(units),
        grad_weight_out,
        small[52],
    )


def solution(mesh):
    in_specs = (
        P("dp", None, "chan"),
        P("dp", None),
        P(),
        P(None, None, "chan"),
        P("chan"),
        P("chan"),
        P("chan"),
        P(None, "chan"),
        P("chan"),
        P("chan", None),
        P("chan"),
        P("dp", None, "chan"),
    )
    out_specs = (
        P("dp", None, "chan"),
        P("dp", None, "chan"),
        P(None, None, "chan"),
        P("chan"),
        P("chan"),
        P("chan"),
        P(None, "chan"),
        P("chan"),
        P("chan", None),
        P("chan"),
    )
    return jax.shard_map(body, mesh=mesh, in_specs=in_specs, out_specs=out_specs, check_vma=False)
```
